32 devices in a mesh: avg: 4 (over x, core), space: 8 (over z, y).
Axes of the slice: x: 2, y: 2, z: 4, core: 2. Of those that a mesh axis runs over, the one named last changes fastest.
Arguments:
- spectral_state: float32 [3, 2, 1024, 1024], P(None, None, 'space', 'avg'), may hold values from -6 to 6
- phase_index: int32 [4], P('avg'), may hold values from 0 to 63
- weight_count: int32 [4], P('avg'), may hold values from 1 to 7
Outputs:
- advanced: float32 [3, 2, 1024, 1024], P(None, None, 'space', 'avg')
The draws below stay inside these ranges and needn't reach their ends.
All inputs are finite; a program needn't handle non-finite values.
Results may differ from the reference program's by a relative error of at most 0.015.
Values may be sent and summed in bfloat16 or wider, within the bound.
A program may use at most 64 MiB of HBM per device.

```python
import jax
import jax.numpy as jnp
from jax import lax

N = 1024
PHASES = 4


def set_ends(drawn, rng, low, largest):
    shape = drawn.shape
    spot = [jax.random.randint(jax.random.fold_in(rng, axis), (), 0, shape[axis]) for axis in range(len(shape))]
    drawn = drawn.at[tuple(spot)].set(low)
    longest = shape.index(max(shape))
    spot[longest] = (spot[longest] + 1) % shape[longest]
    return drawn.at[tuple(spot)].set(largest)


def levels(own_key, dims, shards, low, high):
    factor_of, own = 1.0, jax.random.fold_in(own_key, 6)
    for position, shards_of in shards:
        steps = jnp.exp(jax.random.uniform(jax.random.fold_in(own, position), (shards_of,), jnp.float32, low / len(shards), high / len(shards)))
        factor_of = factor_of * jnp.repeat(steps, dims[position] // shards_of).reshape([-1 if axis == position else 1 for axis in range(len(dims))])
    return factor_of


def scatter_about(own_key, shape, deviation, reach, cuts=(), kind=jnp.bfloat16):
    gain = levels(own_key, shape, cuts, -0.22, 0.18) if cuts else 1.0
    drawn = jax.random.normal(own_key, shape, jnp.float32) * deviation * gain
    return jnp.minimum(jnp.maximum(drawn, -reach), reach).astype(kind)


def setup_inputs(seed: int = 0) -> dict:
    splits = jax.random.split(jax.random.key(seed), 4)
    return {
        "spectral_state": scatter_about(splits[0], (3, 2, N, N), 1.0, 6.0, ((2, 8), (3, 4)), jnp.float32),
        "phase_index": set_ends(jax.random.randint(splits[1], (PHASES,), 0, 64), jax.random.fold_in(splits[1], 1), 0, 63).astype(jnp.int32),
        "weight_count": set_ends(jax.random.randint(splits[2], (PHASES,), 1, 8), jax.random.fold_in(splits[2], 1), 1, 7).astype(jnp.int32),
    }


coriolis = 1.0
wave_speed = 6.0
phase_step = 0.25
time_step = 2.0
weight_scale = 4.0

def wavenumbers(length):
    positions = jnp.arange(length, dtype=jnp.int32)
    shifted = (positions + length // 2) % length - length // 2
    return shifted.astype(jnp.float32) * (2.0 / length)

def wave_operator(fields, wave_rows, wave_columns):
    east_real, north_real, height_real = (fields[0, 0], fields[1, 0], fields[2, 0])
    east_imag, north_imag, height_imag = (fields[0, 1], fields[1, 1], fields[2, 1])
    real_part = jnp.stack([coriolis * north_real + wave_speed * wave_rows * height_imag, -coriolis * east_real + wave_speed * wave_columns * height_imag, wave_speed * (wave_rows * east_imag + wave_columns * north_imag)])
    imag_part = jnp.stack([coriolis * north_imag - wave_speed * wave_rows * height_real, -coriolis * east_imag - wave_speed * wave_columns * height_real, -wave_speed * (wave_rows * east_real + wave_columns * north_real)])
    return jnp.stack([real_part, imag_part], axis=1)

def wave_exponential(fields, wave_rows, wave_columns, phase_value):
    frequency = jnp.sqrt(coriolis * coriolis + wave_speed * wave_speed * (wave_rows * wave_rows + wave_columns * wave_columns))
    sine_term = jnp.sin(frequency * phase_value) / frequency
    cosine_term = (1.0 - jnp.cos(frequency * phase_value)) / (frequency * frequency)
    single = wave_operator(fields, wave_rows, wave_columns)
    double = wave_operator(single, wave_rows, wave_columns)
    return fields + sine_term * single + cosine_term * double

def flux_tendency(spectra, wave_rows, wave_columns):
    real_part, imag_part = (spectra[:, 0], spectra[:, 1])

    def divergence(planes):
        flux_east = jnp.stack([planes[0], planes[1], planes[3]])
        flux_north = jnp.stack([planes[1], planes[2], planes[4]])
        return wave_rows * flux_east + wave_columns * flux_north
    return jnp.stack([divergence(imag_part), -divergence(real_part)], axis=1)

def rounded(values):
    return lax.optimization_barrier(values.astype(jnp.bfloat16)).astype(jnp.float32)

def rounded_complex(values):
    return lax.complex(rounded(values.real), rounded(values.imag))

def reference(spectral_state, phase_index, weight_count):
    wave_table = wavenumbers(N)
    wave_rows = wave_table[:, None]
    wave_columns = wave_table[None, :]
    total_phases = phase_index.shape[0]

    def one_phase(running_sum, inputs):
        sample_index, numerator = inputs
        phase_value = sample_index.astype(jnp.float32) * phase_step
        weight_value = numerator.astype(jnp.float32) / (weight_scale * total_phases)
        rotated = rounded(wave_exponential(spectral_state, wave_rows, wave_columns, phase_value))
        spectral = lax.complex(rotated[:, 0], rotated[:, 1])
        half_done = rounded_complex(jnp.fft.ifft(spectral, axis=2) * N)
        physical = jnp.fft.ifft(half_done, axis=1).real
        east_wind, north_wind, height = (physical[0], physical[1], physical[2])
        products = rounded(jnp.stack([east_wind * east_wind, east_wind * north_wind, north_wind * north_wind, east_wind * height, north_wind * height]))
        forward_half = rounded_complex(jnp.fft.fft(products, axis=1))
        spectra = jnp.fft.fft(forward_half, axis=2) / N
        stacked = jnp.stack([spectra.real, spectra.imag], axis=1)
        tendency = flux_tendency(stacked, wave_rows, wave_columns)
        rotated_back = wave_exponential(tendency, wave_rows, wave_columns, -phase_value)
        return (running_sum + weight_value * rotated_back, None)
    running_sum, unused = lax.scan(one_phase, jnp.zeros(spectral_state.shape, jnp.float32), (phase_index, weight_count))
    return wave_exponential(spectral_state + time_step * running_sum, wave_rows, wave_columns, time_step)
```

```python
import jax
import jax.numpy as jnp
import ml_dtypes
import numpy as np
from jax import lax
from jax.sharding import PartitionSpec as P

coriolis = 1.0
wave_speed = 6.0
phase_step = 0.25
time_step = 2.0
weight_scale = 4.0


def wave_of(positions, length):
    shifted = (positions + length // 2) % length - length // 2
    return shifted.astype(jnp.float32) * (2.0 / length)


def circle(products, length):
    angles = (products % length) * (2.0 * np.pi / length)
    return np.cos(angles).astype(np.float32), np.sin(angles).astype(np.float32)


def slot_base(slot, slots, half):
    return np.where(slot < slots // 2, 2 * half * slot, 2 * half * (slots - 1 - slot) + half)


def packed_table(length, slots):
    half = length // (2 * slots)
    rows = slot_base(np.arange(slots), slots, half)[:, None] + np.arange(half)
    cosine, sine = circle(rows[:, :, None] * np.arange(length), length)
    packed = np.stack([cosine, -sine], axis=1)
    packed[0, 1, 0] = circle(length // 2 * np.arange(length), length)[0]
    return packed.astype(ml_dtypes.bfloat16)


def turned(first, second):
    (c, s), (d, t) = first, second
    return c * d - s * t, s * d + c * t


def column_tables(length, width, groups, order):
    fine = 1
    while fine * fine < width:
        fine *= 2
    y = np.arange(length)
    low = circle(np.arange(fine)[:, None] * y, length)
    high = circle(fine * np.arange(width // fine)[:, None] * y, length)
    block = circle(width * np.arange(groups)[:, None] * y, length)
    low = [jnp.asarray(v)[None, :, :] for v in low]
    high = [jnp.asarray(v)[:, None, :] for v in high]
    inner = [v.reshape(1, width, length) for v in turned(high, low)]
    outer = [jnp.take(jnp.asarray(v), order, axis=0)[:, None, :] for v in block]
    both = [v.reshape(groups * width, length).astype(jnp.bfloat16) for v in turned(outer, inner)]
    return lax.optimization_barrier(tuple(both))


def wave_operator(fields, kx, ky):
    (er, ei), (nr, ni), (hr, hi) = fields
    cx, cy = wave_speed * kx, wave_speed * ky
    return (
        (coriolis * nr + cx * hi, coriolis * ni - cx * hr),
        (cy * hi - coriolis * er, -coriolis * ei - cy * hr),
        (cx * ei + cy * ni, -(cx * er + cy * nr)),
    )


def wave_factors(kx, ky, phase):
    square = coriolis * coriolis + wave_speed * wave_speed * (kx * kx + ky * ky)
    frequency = jnp.sqrt(square)
    angle = frequency * phase
    return jnp.sin(angle) / frequency, (1.0 - jnp.cos(angle)) / square


def wave_exponential(fields, kx, ky, factors):
    sine, cosine = factors
    single = wave_operator(fields, kx, ky)
    double = wave_operator(single, kx, ky)
    return tuple(
        tuple(w + sine * a + cosine * b for w, a, b in zip(ws, one, two))
        for ws, one, two in zip(fields, single, double)
    )


def planes(fields):
    return tuple((fields[i, 0], fields[i, 1]) for i in range(fields.shape[0]))


def per_device(spectral_state, phase_index, weight_count):
    slots, owners = lax.axis_size("space"), lax.axis_size("avg")
    block, width = spectral_state.shape[2:]
    length, half = block * slots, block // 2
    chips = owners // 2
    g, a = lax.axis_index("space"), lax.axis_index("avg")
    low = g < slots // 2
    phase = phase_index[0].astype(jnp.float32) * phase_step
    weight = weight_count[0].astype(jnp.float32) / (weight_scale * owners)

    xor = jnp.array([2 * m + c for c in range(2) for m in range(chips)], jnp.int32)
    order = a ^ xor
    columns = (order[:, None] * width + jnp.arange(width, dtype=jnp.int32)).reshape(1, -1)
    ky = wave_of(columns, length)
    cosine_table, sine_table = column_tables(length, width, owners, order)
    packed = jnp.asarray(packed_table(length, slots))

    base = jnp.where(low, 2 * half * g, 2 * half * (slots - 1 - g) + half)
    direct = base + jnp.arange(half, dtype=jnp.int32)
    mirror = jnp.where(direct == 0, length // 2, length - direct)
    kx = wave_of(jnp.concatenate([direct, mirror])[:, None], length)
    self_paired = (direct == 0)[:, None]

    def flip(values, step):
        return lax.ppermute(values, "avg", [(i, i ^ step) for i in range(owners)])

    swap = [(i, slots - 1 - i) for i in range(slots)]
    edge = [(0, slots // 2)] + [(i, slots - i) for i in range(1, slots // 2)]

    r = np.arange(half)
    into = np.zeros((2, block, half + 8 + block), np.float32)
    into[0, r, half + 8 + r] = 1
    into[0, half + r[1:], half - r[1:]] = 1
    into[0, half, half] = 1
    into[1, r, r] = 1
    into[1, half + r, half + 8 + half - r] = 1
    into = jnp.where(low, into[0], into[1]).astype(jnp.bfloat16)
    narrow = spectral_state.astype(jnp.bfloat16)
    received = lax.ppermute(narrow[:, :, half:], "space", swap)
    corner = lax.ppermute(narrow[:, :, :8], "space", [(t, s) for s, t in edge])
    rows = jnp.concatenate([received, corner, narrow], axis=2)
    mine = jnp.einsum("rk,fckn->fcrn", into, rows, preferred_element_type=jnp.float32)
    mine = mine.astype(jnp.bfloat16)
    same = jnp.concatenate([mine] + [flip(mine, 2 * m) for m in range(1, chips)], axis=3)
    gathered = jnp.concatenate([same, flip(same, 1)], axis=3).astype(jnp.float32)

    forward_factors = lax.optimization_barrier(wave_factors(kx, ky, phase))
    rotated = wave_exponential(planes(gathered), kx, ky, forward_factors)
    cosine_rows, sine_rows = [], []
    parts = []
    for real, imag in rotated:
        re1, re2 = real[:half], real[half:]
        im1, im2 = imag[:half], imag[half:]
        parts.append((
            jnp.where(self_paired, re1, re1 + re2),
            jnp.where(self_paired, re2, im1 - im2),
            jnp.where(self_paired, -im1, -(im1 + im2)),
            jnp.where(self_paired, -im2, re1 - re2),
        ))
    cosine_rows = jnp.stack([jnp.stack([p[c] for p in parts]) for c in range(2)]).astype(jnp.bfloat16)
    sine_rows = jnp.stack([jnp.stack([p[2 + c] for p in parts]) for c in range(2)]).astype(jnp.bfloat16)
    half_done = (
        jnp.einsum("cfkn,ny->cfky", cosine_rows, cosine_table, preferred_element_type=jnp.float32)
        + jnp.einsum("cfkn,ny->cfky", sine_rows, sine_table, preferred_element_type=jnp.float32)
    ).astype(jnp.bfloat16)
    outgoing = half_done.reshape(2, 3, half, slots, block).transpose(3, 0, 1, 2, 4)
    arrived = lax.all_to_all(outgoing, "space", split_axis=0, concat_axis=0, tiled=True)
    physical = jnp.einsum(
        "pckx,pcfky->xfy", packed, arrived, preferred_element_type=jnp.float32
    ) * (1.0 / length)
    east, north, height = physical[:, 0], physical[:, 1], physical[:, 2]
    products = jnp.stack(
        [east * east, east * north, north * north, east * height, north * height], axis=1
    ).astype(jnp.bfloat16)
    forward_half = jnp.einsum(
        "gcrx,xqy->gcrqy", packed, products, preferred_element_type=jnp.float32
    ).astype(jnp.bfloat16)
    returned = lax.all_to_all(forward_half, "space", split_axis=0, concat_axis=0, tiled=True)
    returned = returned.transpose(3, 1, 2, 0, 4).reshape(5, 2, half, length)
    by_cosine = jnp.einsum(
        "qcry,ny->qcrn", returned, cosine_table, preferred_element_type=jnp.float32
    )
    by_sine = jnp.einsum(
        "qcry,ny->qcrn", returned, sine_table, preferred_element_type=jnp.float32
    )
    rc, ic = by_cosine[:, 0], by_cosine[:, 1]
    rs, isn = by_sine[:, 0], by_sine[:, 1]
    scale = weight / length
    real = scale * jnp.concatenate(
        [jnp.where(self_paired, rc, rc + isn), jnp.where(self_paired, ic, rc - isn)], axis=1
    )
    imag = scale * jnp.concatenate(
        [jnp.where(self_paired, -rs, ic - rs), jnp.where(self_paired, -isn, -ic - rs)], axis=1
    )
    tendency = tuple(
        (kx * imag[i] + ky * imag[j], -(kx * real[i] + ky * real[j]))
        for i, j in ((0, 1), (1, 2), (3, 4))
    )
    back = wave_exponential(tendency, kx, ky, (-forward_factors[0], forward_factors[1]))
    back = jnp.stack([jnp.stack(p) for p in back]).astype(jnp.bfloat16)

    split = chips * width
    near = back[..., :split].astype(jnp.float32) + flip(back[..., split:], 1).astype(jnp.float32)
    sent = near.astype(jnp.bfloat16)
    total = near[..., :width]
    for m in range(1, chips):
        total = total + flip(sent[..., m * width : (m + 1) * width], 2 * m).astype(jnp.float32)
    summed = total.astype(jnp.bfloat16)

    out = np.zeros((2, block, half + half + 8), np.float32)
    out[0, r, r] = 1
    out[0, half + r, half + r] = 1
    out[1, half - r, r] = 1
    out[1, block - r[1:], half + r[1:]] = 1
    out[1, 0, 2 * half] = 1
    out = jnp.where(low, out[0], out[1]).astype(jnp.bfloat16)
    first, second = summed[:, :, :half], summed[:, :, half:]
    own = jnp.where(low, first, second)
    other = lax.ppermute(jnp.where(low, second, first), "space", swap)
    corner = lax.ppermute(second[:, :, :8], "space", edge)
    rows = jnp.concatenate([own, other, corner], axis=2)
    averaged = jnp.einsum("rk,fckn->fcrn", out, rows, preferred_element_type=jnp.float32)

    own_rows = wave_of(g * block + jnp.arange(block, dtype=jnp.int32)[:, None], length)
    own_columns = ky[:, :width]
    state = spectral_state + time_step * averaged
    factors = wave_factors(own_rows, own_columns, time_step)
    advanced = wave_exponential(planes(state), own_rows, own_columns, factors)
    return jnp.stack([jnp.stack(p) for p in advanced])


def solution(mesh):
    in_specs = (P(None, None, "space", "avg"), P("avg"), P("avg"))
    out_specs = P(None, None, "space", "avg")
    return jax.shard_map(
        per_device, mesh=mesh, in_specs=in_specs, out_specs=out_specs, check_vma=False
    )
```

```python
import functools

import jax
import jax.numpy as jnp
import ml_dtypes
import numpy as np
from jax import lax
from jax.experimental import pallas as pl
from jax.experimental.pallas import tpu as pltpu
from jax.sharding import PartitionSpec as P

coriolis = 1.0
wave_speed = 6.0
phase_step = 0.25
time_step = 2.0
weight_scale = 4.0


def wave_of(positions, length):
    shifted = (positions + length // 2) % length - length // 2
    return shifted.astype(jnp.float32) * (2.0 / length)


def circle(products, length):
    angles = (products % length) * (2.0 * np.pi / length)
    return np.cos(angles).astype(np.float32), np.sin(angles).astype(np.float32)


def slot_base(slot, slots, half):
    return np.where(slot < slots // 2, 2 * half * slot, 2 * half * (slots - 1 - slot) + half)


def packed_table(length, slots, chunks):
    half = length // (2 * slots)
    rows = slot_base(np.arange(slots), slots, half)[:, None] + np.arange(half)
    cosine, sine = circle(rows[:, :, None] * np.arange(length), length)
    packed = np.stack([cosine, -sine], axis=1)
    packed[0, 1, 0] = circle(length // 2 * np.arange(length), length)[0]
    packed = packed.reshape(slots, 2, chunks, half // chunks, length).transpose(2, 0, 1, 3, 4)
    return packed.reshape(length, length).astype(ml_dtypes.bfloat16)


def turned(first, second):
    (c, s), (d, t) = first, second
    return c * d - s * t, s * d + c * t


def column_tables(length, width, groups, order):
    fine = 1
    while fine * fine < width:
        fine *= 2
    y = np.arange(length)
    low = circle(np.arange(fine)[:, None] * y, length)
    high = circle(fine * np.arange(width // fine)[:, None] * y, length)
    block = circle(width * np.arange(groups)[:, None] * y, length)
    low = [jnp.asarray(v)[None, :, :] for v in low]
    high = [jnp.asarray(v)[:, None, :] for v in high]
    inner = [v.reshape(1, width, length) for v in turned(high, low)]
    outer = [jnp.take(jnp.asarray(v), order, axis=0)[:, None, :] for v in block]
    both = [v.reshape(groups * width, length).astype(jnp.bfloat16) for v in turned(outer, inner)]
    return lax.optimization_barrier(tuple(both))


def wave_operator(fields, kx, ky):
    (er, ei), (nr, ni), (hr, hi) = fields
    cx, cy = wave_speed * kx, wave_speed * ky
    return (
        (coriolis * nr + cx * hi, coriolis * ni - cx * hr),
        (cy * hi - coriolis * er, -coriolis * ei - cy * hr),
        (cx * ei + cy * ni, -(cx * er + cy * nr)),
    )


def wave_factors(kx, ky, phase):
    square = coriolis * coriolis + wave_speed * wave_speed * (kx * kx + ky * ky)
    frequency = jnp.sqrt(square)
    angle = frequency * phase
    return jnp.sin(angle) / frequency, (1.0 - jnp.cos(angle)) / square


def wave_exponential(fields, kx, ky, factors):
    sine, cosine = factors
    single = wave_operator(fields, kx, ky)
    double = wave_operator(single, kx, ky)
    return tuple(
        tuple(w + sine * a + cosine * b for w, a, b in zip(ws, one, two))
        for ws, one, two in zip(fields, single, double)
    )


def planes(fields):
    return tuple((fields[i, 0], fields[i, 1]) for i in range(fields.shape[0]))


MESH = pl.DeviceIdType.MESH
EDGE = 16


def column(info, t, index):
    return info[t, :, index : index + 1]


def positions():
    g, a = lax.axis_index("space"), lax.axis_index("avg")
    return g, a, a // 2, a % 2


def edge_partner(g, slots):
    aligned = 1 - (g % (slots // 2) + slots // 2 - 1) // (slots // 2)
    return ((slots - g) % slots + aligned * (slots // 2)) % slots


def greet(slots, chips, edges):
    g, a, q, core = positions()
    barrier = pltpu.get_barrier_semaphore()
    peers = [((g + d) % slots, a) for d in range(1, slots)]
    peers += [(g, 2 * q + 1 - core)]
    peers += [(g, 2 * ((q + m) % chips) + core) for m in range(1, chips)]
    if edges:
        across = edge_partner(g, slots)
        peers += [
            (across, 2 * ((q + m) % chips) + (core + c) % 2)
            for c in range(2) for m in range(chips) if c or m
        ]
    for space, avg in peers:
        pl.semaphore_signal(
            barrier, inc=1, device_id={"space": space, "avg": avg}, device_id_type=MESH
        )
    pl.semaphore_wait(barrier, len(peers))


def remote(src, dst, send, recv, space, avg):
    return pltpu.make_async_remote_copy(
        src_ref=src, dst_ref=dst, send_sem=send, recv_sem=recv,
        device_id={"space": space, "avg": avg}, device_id_type=MESH,
    )


def forward_kernel(
    dims, keep, send, edge, sine, cosine, info, ky, ct, st, out,
    gx, eg, rows_c, rows_s, stage,
    ex_s, ex_r, eg_s, eg_r, x_s, x_r, c_s, c_r, a_s, a_r, l_s,
):
    slots, chips, chunks, hb, width, block = dims
    length = slots * block
    g, a, q, core = positions()
    low, high = g < slots // 2, g >= slots // 2
    partner = 2 * q + 1 - core
    across = edge_partner(g, slots)
    greet(slots, chips, True)

    exchange = [
        remote(send.at[t], gx.at[t, 1, 0, 0], ex_s.at[t], ex_r.at[t], slots - 1 - g, a)
        for t in range(chunks)
    ]
    edges = [
        remote(edge, eg.at[c, m], eg_s.at[c, m], eg_r.at[c, m],
               across, 2 * ((q + chips - m) % chips) + (core + c) % 2)
        for c in range(2) for m in range(chips)
    ]

    def mine(t, s):
        return gx.at[t, 1, 0, 0] if s else keep.at[t]

    def over_chips(t, s, m):
        return remote(mine(t, s), gx.at[t, s, 0, m], x_s.at[t, s, m], x_r.at[t, s, m],
                      g, 2 * ((q + chips - m) % chips) + core)

    def over_cores(t, s, m):
        source = gx.at[t, s, 0, m] if m else mine(t, s)
        return remote(source, gx.at[t, s, 1, m], c_s.at[t, s, m], c_r.at[t, s, m], g, partner)

    def all_to_all(t, d):
        to = (g + d) % slots
        return remote(stage.at[t, to], out.at[t, g], a_s.at[t, d], a_r.at[t, d], to, a)

    exchange[0].start()

    @pl.when(high)
    def _():
        for copy in edges:
            copy.start()
        eg[...] = jnp.zeros_like(eg)

    for t in range(1, chunks):
        exchange[t].start()
    for t in range(chunks):
        for m in range(1, chips):
            over_chips(t, 0, m).start()
        over_cores(t, 0, 0).start()
    for t in range(chunks):
        for m in range(1, chips):
            over_chips(t, 0, m).wait_recv()
            over_cores(t, 0, m).start()
    for t in range(chunks):
        exchange[t].wait_recv()
        for m in range(1, chips):
            over_chips(t, 1, m).start()
        over_cores(t, 1, 0).start()
        for m in range(1, chips):
            over_chips(t, 1, m).wait_recv()
            over_cores(t, 1, m).start()
        if t == 0:
            @pl.when(low)
            def _():
                for copy in edges:
                    copy.wait_recv()
        for s in range(2):
            for m in range(chips):
                over_cores(t, s, m).wait_recv()
        own_pair = column(info, t, 2) > 0.5
        sign = column(info, t, 3)
        for j in range(2 * chips):
            c, m = divmod(j, chips)
            span = slice(j * width, (j + 1) * width)
            turned_rows = []
            for s in range(2):
                source = keep.at[t] if s + j == 0 else gx.at[t, s, c, m]
                fields = [[source[f, i].astype(jnp.float32) for i in range(2)] for f in range(3)]
                if s == 1 and t == 0:
                    put = column(info, t, 4)[:EDGE] > 0.5
                    for f in range(3):
                        for i in range(2):
                            top = jnp.where(put, eg[c, m, f, i].astype(jnp.float32), fields[f][i][:EDGE])
                            fields[f][i] = (
                                jnp.concatenate([top, fields[f][i][EDGE:]], axis=0) if hb > EDGE else top
                            )
                turned_rows.append(wave_exponential(
                    fields, column(info, t, s), ky[:, span], (sine[t, s, :, span], cosine[t, s, :, span])
                ))
            for f in range(3):
                (re0, im0), (re1, im1) = turned_rows[0][f], turned_rows[1][f]
                for i, value in enumerate((
                    jnp.where(own_pair, re0, re0 + re1), jnp.where(own_pair, re1, sign * (im0 - im1))
                )):
                    rows_c[(i * 3 + f) * hb : (i * 3 + f + 1) * hb, span] = value.astype(jnp.bfloat16)
                for i, value in enumerate((
                    jnp.where(own_pair, -im0, -(im0 + im1)), jnp.where(own_pair, -im1, sign * (re0 - re1))
                )):
                    rows_s[(i * 3 + f) * hb : (i * 3 + f + 1) * hb, span] = value.astype(jnp.bfloat16)
        tile = min(length, max(block, 256))
        for y in range(0, length, tile):
            value = (
                jnp.dot(rows_c[...], ct[:, y : y + tile], preferred_element_type=jnp.float32)
                + jnp.dot(rows_s[...], st[:, y : y + tile], preferred_element_type=jnp.float32)
            ).astype(jnp.bfloat16)
            for b in range(tile // block):
                for i in range(2):
                    for f in range(3):
                        stage[t, y // block + b, i * hb : (i + 1) * hb, f * block : (f + 1) * block] = (
                            value[(i * 3 + f) * hb : (i * 3 + f + 1) * hb, b * block : (b + 1) * block]
                        )
        for d in range(1, slots):
            all_to_all(t, d).start()
        pltpu.make_async_copy(stage.at[t, g], out.at[t, g], l_s.at[t]).start()
    for t in range(chunks):
        for d in range(1, slots):
            all_to_all(t, d).wait_recv()
        pltpu.make_async_copy(stage.at[t, g], out.at[t, g], l_s.at[t]).wait()
    for t in range(chunks):
        exchange[t].wait_send()
        for s in range(2):
            for m in range(1, chips):
                over_chips(t, s, m).wait_send()
            for m in range(chips):
                over_cores(t, s, m).wait_send()
        for d in range(1, slots):
            all_to_all(t, d).wait_send()

    @pl.when(high)
    def _():
        for copy in edges:
            copy.wait_send()


def backward_kernel(
    dims, fh, sine, cosine, info, ky, ct, st, own, other, edge,
    ret, lhs, stage, rsin, acc, xs, rx, fin,
    a_s, a_r, l_s, c_s, c_r, x_s, x_r, ex_s, ex_r, eg_s, eg_r,
):
    slots, chips, chunks, hb, width, block = dims
    g, a, q, core = positions()
    low, high = g < slots // 2, g >= slots // 2
    partner = 2 * q + 1 - core
    greet(slots, chips, False)

    def all_to_all(t, d):
        to = (g + d) % slots
        return remote(fh.at[t, to], ret.at[t, g], a_s.at[t, d], a_r.at[t, d], to, a)

    def over_cores(t):
        return remote(stage.at[t, 1], rsin.at[t], c_s.at[t], c_r.at[t], g, partner)

    def over_chips(t, m):
        return remote(xs.at[t, m], rx.at[t, m], x_s.at[t, m], x_r.at[t, m],
                      g, 2 * ((q + m) % chips) + core)

    def exchange(t):
        return remote(fin.at[t], other.at[t], ex_s.at[t], ex_r.at[t], slots - 1 - g, a)

    edges = remote(fin.at[0, :, :, :EDGE], edge, eg_s, eg_r, edge_partner(g, slots), a)

    for t in range(chunks):
        for d in range(1, slots):
            all_to_all(t, d).start()
        pltpu.make_async_copy(fh.at[t, g], ret.at[t, g], l_s.at[t]).start()

    @pl.when(low)
    def _():
        edge[...] = jnp.zeros_like(edge)

    for t in range(chunks):
        for d in range(1, slots):
            all_to_all(t, d).wait_recv()
        pltpu.make_async_copy(fh.at[t, g], ret.at[t, g], l_s.at[t]).wait()
        for p in range(slots):
            for k in range(5):
                lhs[k * 2 * hb : (k + 1) * 2 * hb, p * block : (p + 1) * block] = (
                    ret[t, p, :, k * block : (k + 1) * block]
                )
        own_pair = column(info, t, 2) > 0.5
        sign, scale = column(info, t, 3), column(info, t, 5)
        for j in range(2 * chips):
            c, m = divmod(j, chips)
            span = slice(j * width, (j + 1) * width)
            dims_nt = (((1,), (1,)), ((), ()))
            by_c = lax.dot_general(lhs[...], ct[span, :], dims_nt, preferred_element_type=jnp.float32)
            by_s = lax.dot_general(lhs[...], st[span, :], dims_nt, preferred_element_type=jnp.float32)

            def part(values, k, i):
                return values[(2 * k + i) * hb : (2 * k + i + 1) * hb]

            for s in range(2):
                turn = scale * sign if s == 0 else -scale * sign
                real, imag = [], []
                for k in range(5):
                    rc, ic = part(by_c, k, 0), part(by_c, k, 1)
                    rs, iz = part(by_s, k, 0), part(by_s, k, 1)
                    real.append(jnp.where(own_pair, scale * (ic if s else rc), scale * rc + turn * iz))
                    imag.append(jnp.where(own_pair, -scale * (iz if s else rs), turn * ic - scale * rs))
                kx, kyj = column(info, t, s), ky[:, span]
                tendency = [
                    (kx * imag[u] + kyj * imag[v], -(kx * real[u] + kyj * real[v]))
                    for u, v in ((0, 1), (1, 2), (3, 4))
                ]
                back = wave_exponential(
                    tendency, kx, kyj, (-sine[t, s, :, span], cosine[t, s, :, span])
                )
                for f in range(3):
                    for i in range(2):
                        stage[t, c, m, s, f, i] = back[f][i].astype(jnp.bfloat16)
        over_cores(t).start()
        over_cores(t).wait_recv()
        for m in range(1, chips):
            xs[t, m] = (
                stage[t, 0, m].astype(jnp.float32) + rsin[t, m].astype(jnp.float32)
            ).astype(jnp.bfloat16)
            over_chips(t, m).start()
        acc[...] = stage[t, 0, 0].astype(jnp.float32) + rsin[t, 0].astype(jnp.float32)
        for m in range(1, chips):
            over_chips(t, m).wait_recv()
            acc[...] += rx[t, m].astype(jnp.float32)
        fin[t] = acc[1].astype(jnp.bfloat16)
        exchange(t).start()
        if t == 0:
            @pl.when(low)
            def _():
                edges.start()
        own[t] = acc[0].astype(jnp.bfloat16)
    for t in range(chunks):
        exchange(t).wait_recv()

    @pl.when(high)
    def _():
        edges.wait_recv()

    for t in range(chunks):
        for d in range(1, slots):
            all_to_all(t, d).wait_send()
        over_cores(t).wait_send()
        for m in range(1, chips):
            over_chips(t, m).wait_send()
        exchange(t).wait_send()

    @pl.when(low)
    def _():
        edges.wait_send()


VMEM = pl.BlockSpec(memory_space=pltpu.VMEM)


def per_device(spectral_state, phase_index, weight_count):
    slots, owners = lax.axis_size("space"), lax.axis_size("avg")
    block, width = spectral_state.shape[2:]
    length, half = block * slots, block // 2
    chips = owners // 2
    chunks = max(1, half // CHUNK_ROWS)
    hb = half // chunks
    dims = (slots, chips, chunks, hb, width, block)
    g, a = lax.axis_index("space"), lax.axis_index("avg")
    q, core = a // 2, a % 2
    low = g < slots // 2
    phase = phase_index[0].astype(jnp.float32) * phase_step
    weight = weight_count[0].astype(jnp.float32) / (weight_scale * owners)

    m, c = jnp.arange(chips, dtype=jnp.int32), jnp.arange(2, dtype=jnp.int32)[:, None]
    order = (2 * ((q + m) % chips) + (core + c) % 2).reshape(-1)
    columns = (order[:, None] * width + jnp.arange(width, dtype=jnp.int32)).reshape(1, -1)
    ky = wave_of(columns, length)
    cosine_table, sine_table = column_tables(length, width, owners, order)
    packed = jnp.asarray(packed_table(length, slots, chunks))

    base = jnp.where(low, 2 * half * g, 2 * half * (slots - 1 - g) + half)
    direct = base + jnp.arange(half, dtype=jnp.int32)
    mirror = jnp.where(direct == 0, length // 2, length - direct)
    first = wave_of(jnp.where(low, direct, mirror), length)
    second = wave_of(jnp.where(low, mirror, direct), length)
    ones = jnp.ones((half,), jnp.float32)
    start = (jnp.arange(half) == 0) & low
    info = jnp.stack([
        first, second, (direct == 0).astype(jnp.float32), jnp.where(low, ones, -ones),
        start.astype(jnp.float32), ones * (weight / length), ones, ones,
    ], axis=1).reshape(chunks, hb, 8)
    rows = jnp.stack([first, second]).reshape(2, chunks, hb).transpose(1, 0, 2)[..., None]
    sine, cosine = lax.optimization_barrier(wave_factors(rows, ky, phase))

    r = np.arange(half)
    into = np.zeros((2, 2, half, block), np.float32)
    into[0, 0, r, r] = 1
    into[0, 1, r, half + r] = 1
    into[1, 0, r, half - r] = 1
    into[1, 1, r[1:], block - r[1:]] = 1
    into = jnp.where(low, into[0], into[1]).astype(jnp.bfloat16).reshape(2, chunks, hb, block)
    narrow = spectral_state.astype(jnp.bfloat16)
    pick = lambda which: jnp.einsum(
        "thk,fckn->tfchn", into[which], narrow, preferred_element_type=jnp.float32
    ).astype(jnp.bfloat16)
    keep, send = pick(0), pick(1)

    piece = (3, 2, hb, width)
    dma = pltpu.SemaphoreType.DMA
    vmem = lambda shape: pltpu.VMEM(shape, jnp.bfloat16)
    arrived = pl.pallas_call(
        functools.partial(forward_kernel, dims),
        out_shape=jax.ShapeDtypeStruct((chunks, slots, 2 * hb, 3 * block), jnp.bfloat16),
        in_specs=[VMEM] * 9,
        out_specs=VMEM,
        scratch_shapes=[
            vmem((chunks, 2, 2, chips) + piece),
            vmem((2, chips, 3, 2, EDGE, width)),
            vmem((6 * hb, length)),
            vmem((6 * hb, length)),
            vmem((chunks, slots, 2 * hb, 3 * block)),
            dma((chunks,)), dma((chunks,)),
            dma((2, chips)), dma((2, chips)),
            dma((chunks, 2, chips)), dma((chunks, 2, chips)),
            dma((chunks, 2, chips)), dma((chunks, 2, chips)),
            dma((chunks, slots)), dma((chunks, slots)),
            dma((chunks,)),
        ],
        compiler_params=pltpu.CompilerParams(
            collective_id=0, has_side_effects=True, vmem_limit_bytes=48 * 2**20
        ),
        name="spectral_to_grid",
    )(keep, send, narrow[:, :, :EDGE], sine, cosine, info, ky, cosine_table, sine_table)

    physical = lax.dot_general(
        packed, arrived.reshape(length, 3 * block), (((0,), (0,)), ((), ())),
        preferred_element_type=jnp.float32,
    ) * (1.0 / length)
    east, north, height = (physical[:, i * block : (i + 1) * block] for i in range(3))
    products = jnp.concatenate(
        [east * east, east * north, north * north, east * height, north * height], axis=1
    ).astype(jnp.bfloat16)
    forward_half = jnp.dot(packed, products, preferred_element_type=jnp.float32).astype(jnp.bfloat16)
    forward_half = forward_half.reshape(chunks, slots, 2 * hb, 5 * block)

    own, other, edge = pl.pallas_call(
        functools.partial(backward_kernel, dims),
        out_shape=[
            jax.ShapeDtypeStruct((chunks,) + piece, jnp.bfloat16),
            jax.ShapeDtypeStruct((chunks,) + piece, jnp.bfloat16),
            jax.ShapeDtypeStruct((3, 2, EDGE, width), jnp.bfloat16),
        ],
        in_specs=[VMEM] * 7,
        out_specs=[VMEM] * 3,
        scratch_shapes=[
            vmem((chunks, slots, 2 * hb, 5 * block)),
            vmem((10 * hb, length)),
            vmem((chunks, 2, chips, 2) + piece),
            vmem((chunks, chips, 2) + piece),
            pltpu.VMEM((2,) + piece, jnp.float32),
            vmem((chunks, chips, 2) + piece),
            vmem((chunks, chips, 2) + piece),
            vmem((chunks,) + piece),
            dma((chunks, slots)), dma((chunks, slots)), dma((chunks,)),
            dma((chunks,)), dma((chunks,)),
            dma((chunks, chips)), dma((chunks, chips)),
            dma((chunks,)), dma((chunks,)),
            dma(()), dma(()),
        ],
        compiler_params=pltpu.CompilerParams(
            collective_id=1, has_side_effects=True, vmem_limit_bytes=48 * 2**20
        ),
        name="grid_to_spectral",
    )(forward_half, sine, cosine, info, ky, cosine_table, sine_table)

    back = np.zeros((2, block, 2 * half + EDGE), np.float32)
    back[0, r, r] = 1
    back[0, half + r, half + r] = 1
    back[1, half - r, r] = 1
    back[1, block - r[1:], half + r[1:]] = 1
    back[1, 0, 2 * half] = 1
    back = jnp.where(low, back[0], back[1]).astype(jnp.bfloat16)
    tall = lambda v: v.transpose(1, 2, 0, 3, 4).reshape(3, 2, half, width)
    stacked = jnp.concatenate([tall(own), tall(other), edge], axis=2)
    averaged = jnp.einsum("rk,fckn->fcrn", back, stacked, preferred_element_type=jnp.float32)

    own_rows = wave_of(g * block + jnp.arange(block, dtype=jnp.int32)[:, None], length)
    own_columns = ky[:, :width]
    state = spectral_state + time_step * averaged
    factors = wave_factors(own_rows, own_columns, time_step)
    advanced = wave_exponential(planes(state), own_rows, own_columns, factors)
    return jnp.stack([jnp.stack(p) for p in advanced])


CHUNK_ROWS = 32


def solution(mesh):
    in_specs = (P(None, None, "space", "avg"), P("avg"), P("avg"))
    out_specs = P(None, None, "space", "avg")
    return jax.shard_map(
        per_device, mesh=mesh, in_specs=in_specs, out_specs=out_specs, check_vma=False
    )
```

```python
import functools

import jax
import jax.numpy as jnp
import ml_dtypes
import numpy as np
from jax import lax
from jax.experimental import pallas as pl
from jax.experimental.pallas import tpu as pltpu
from jax.sharding import PartitionSpec as P

coriolis = 1.0
wave_speed = 6.0
phase_step = 0.25
time_step = 2.0
weight_scale = 4.0


def wave_of(positions, length):
    shifted = (positions + length // 2) % length - length // 2
    return shifted.astype(jnp.float32) * (2.0 / length)


def circle(products, length):
    angles = (products % length) * (2.0 * np.pi / length)
    return np.cos(angles).astype(np.float32), np.sin(angles).astype(np.float32)


def slot_base(slot, slots, half):
    return np.where(slot < slots // 2, 2 * half * slot, 2 * half * (slots - 1 - slot) + half)


def packed_table(length, slots, chunks):
    half = length // (2 * slots)
    rows = slot_base(np.arange(slots), slots, half)[:, None] + np.arange(half)
    cosine, sine = circle(rows[:, :, None] * np.arange(length), length)
    packed = np.stack([cosine, -sine], axis=1)
    packed[0, 1, 0] = circle(length // 2 * np.arange(length), length)[0]
    packed = packed.reshape(slots, 2, chunks, half // chunks, length).transpose(2, 0, 1, 3, 4)
    return packed.reshape(length, length).astype(ml_dtypes.bfloat16)


def turned(first, second):
    (c, s), (d, t) = first, second
    return c * d - s * t, s * d + c * t


def angle_tables(length, width, owners):
    y = np.arange(length)
    return [
        jnp.asarray(np.stack(circle(step * np.arange(count)[:, None] * y, length)))
        for step, count in ((width, owners), (FINE, width // FINE), (1, FINE))
    ]


def wave_operator(fields, kx, ky):
    (er, ei), (nr, ni), (hr, hi) = fields
    cx, cy = wave_speed * kx, wave_speed * ky
    return (
        (coriolis * nr + cx * hi, coriolis * ni - cx * hr),
        (cy * hi - coriolis * er, -coriolis * ei - cy * hr),
        (cx * ei + cy * ni, -(cx * er + cy * nr)),
    )


def wave_factors(kx, ky, phase):
    square = coriolis * coriolis + wave_speed * wave_speed * (kx * kx + ky * ky)
    frequency = jnp.sqrt(square)
    angle = frequency * phase
    return jnp.sin(angle) / frequency, (1.0 - jnp.cos(angle)) / square


def wave_exponential(fields, kx, ky, factors):
    sine, cosine = factors
    single = wave_operator(fields, kx, ky)
    double = wave_operator(single, kx, ky)
    return tuple(
        tuple(w + sine * a + cosine * b for w, a, b in zip(ws, one, two))
        for ws, one, two in zip(fields, single, double)
    )


def planes(fields):
    return tuple((fields[i, 0], fields[i, 1]) for i in range(fields.shape[0]))


MESH = pl.DeviceIdType.MESH
EDGE = 16
FINE = 16


def column(info, t, index):
    return info[t, :, index : index + 1]


def positions():
    g, a = lax.axis_index("space"), lax.axis_index("avg")
    return g, a, a // 2, a % 2


def edge_partner(g, slots):
    aligned = 1 - (g % (slots // 2) + slots // 2 - 1) // (slots // 2)
    return ((slots - g) % slots + aligned * (slots // 2)) % slots


def greet(slots, chips, edges):
    g, a, q, core = positions()
    barrier = pltpu.get_barrier_semaphore()
    peers = [((g + d) % slots, a) for d in range(1, slots)]
    peers += [(g, 2 * q + 1 - core)]
    peers += [(g, 2 * ((q + m) % chips) + core) for m in range(1, chips)]
    if edges:
        across = edge_partner(g, slots)
        peers += [
            (across, 2 * ((q + m) % chips) + (core + c) % 2)
            for c in range(2) for m in range(chips) if c or m
        ]
    for space, avg in peers:
        pl.semaphore_signal(
            barrier, inc=1, device_id={"space": space, "avg": avg}, device_id_type=MESH
        )
    pl.semaphore_wait(barrier, len(peers))


def remote(src, dst, send, recv, space, avg):
    return pltpu.make_async_remote_copy(
        src_ref=src, dst_ref=dst, send_sem=send, recv_sem=recv,
        device_id={"space": space, "avg": avg}, device_id_type=MESH,
    )


DIMS_NT = (((1,), (1,)), ((), ()))


def step_kernel(
    dims, state, into_rows, back_rows, info, ky, own_kx, phase, blocks, steps, fines, packed_hbm, result,
    moved, top, gx, eg, rows_c, rows_s, half, arr, arr_t, grid, products, packed, ct, st, sine, cosine,
    end_sine, end_cosine, fh, ret, lhs, stage, rsin, acc, xs, rx, fin, own, other, edge,
    ex_s, ex_r, eg_s, eg_r, x_s, x_r, c_s, c_r, a_s, a_r, l_s,
    b_s, b_r, m_s, d_s, d_r, y_s, y_r, gv_s, gv_r, le_s, le_r, bring_s,
):
    slots, chips, chunks, hb, width, block = dims
    length, reach = slots * block, block // 2
    g, a, q, core = positions()
    low, high = g < slots // 2, g >= slots // 2
    partner = 2 * q + 1 - core
    across = edge_partner(g, slots)
    bring = pltpu.make_async_copy(packed_hbm, packed, bring_s)

    for f in range(3):
        for i in range(2):
            plane = state[f, i].astype(jnp.bfloat16)
            top[f, i] = plane[:EDGE]
            picked = jnp.dot(into_rows[...], plane, preferred_element_type=jnp.float32)
            picked = picked.astype(jnp.bfloat16)
            for s in range(2):
                for t in range(chunks):
                    spot = s * reach + t * hb
                    moved[s, t, f, i] = picked[spot : spot + hb]
    greet(slots, chips, True)

    def build_factors(unused):
        for t in range(chunks):
            for s in range(2):
                def one(j, carry, t=t, s=s):
                    span = pl.ds(pl.multiple_of(j * 256, 256), 256)
                    factors = wave_factors(column(info, t, s), ky[:, span], phase[...])
                    sine[t, s, :, span], cosine[t, s, :, span] = factors
                    return carry
                lax.fori_loop(0, length // 256, one, 0)

    def own_factors():
        end_sine[...], end_cosine[...] = wave_factors(own_kx[...], ky[:, :width], time_step)

    def build_tables():
        for c in range(2):
            for m in range(chips):
                owner = 2 * ((q + m) % chips) + (core + c) % 2
                first = (blocks[0, pl.ds(owner, 1), :], blocks[1, pl.ds(owner, 1), :])

                def one(h, carry, j=c * chips + m, first=first):
                    begin = turned(first, (steps[0, pl.ds(h, 1), :], steps[1, pl.ds(h, 1), :]))
                    cos_rows, sin_rows = turned(begin, (fines[0], fines[1]))
                    at = pl.ds(pl.multiple_of(j * width + h * FINE, FINE), FINE)
                    ct[at, :] = cos_rows.astype(jnp.bfloat16)
                    st[at, :] = sin_rows.astype(jnp.bfloat16)
                    return carry
                lax.fori_loop(0, width // FINE, one, 0)

    exchange = [
        remote(moved.at[1, t], gx.at[t, 1, 0, 0], ex_s.at[t], ex_r.at[t], slots - 1 - g, a)
        for t in range(chunks)
    ]
    edges = [
        remote(top, eg.at[c, m], eg_s.at[c, m], eg_r.at[c, m],
               across, 2 * ((q + chips - m) % chips) + (core + c) % 2)
        for c in range(2) for m in range(chips)
    ]

    def mine(t, s):
        return gx.at[t, 1, 0, 0] if s else moved.at[0, t]

    def over_chips(t, s, m):
        return remote(mine(t, s), gx.at[t, s, 0, m], x_s.at[t, s, m], x_r.at[t, s, m],
                      g, 2 * ((q + chips - m) % chips) + core)

    def over_cores(t, s, m):
        source = gx.at[t, s, 0, m] if m else mine(t, s)
        return remote(source, gx.at[t, s, 1, m], c_s.at[t, s, m], c_r.at[t, s, m], g, partner)

    def to_grid(t, d):
        to = (g + d) % slots
        return remote(half.at[t, to], arr.at[t, g], a_s.at[t, d], a_r.at[t, d], to, a)

    exchange[0].start()

    @pl.when(high)
    def _():
        for copy in edges:
            copy.start()
        eg[...] = jnp.zeros_like(eg)

    for t in range(1, chunks):
        exchange[t].start()
    for t in range(chunks):
        for m in range(1, chips):
            over_chips(t, 0, m).start()
        over_cores(t, 0, 0).start()
    bring.start()
    build_factors(0)
    build_tables()
    for t in range(chunks):
        for m in range(1, chips):
            over_chips(t, 0, m).wait_recv()
            over_cores(t, 0, m).start()
    for t in range(chunks):
        exchange[t].wait_recv()
        for m in range(1, chips):
            over_chips(t, 1, m).start()
        over_cores(t, 1, 0).start()
        for m in range(1, chips):
            over_chips(t, 1, m).wait_recv()
            over_cores(t, 1, m).start()
        if t == 0:
            @pl.when(low)
            def _():
                for copy in edges:
                    copy.wait_recv()
        for s in range(2):
            for m in range(chips):
                over_cores(t, s, m).wait_recv()
        own_pair = column(info, t, 2) > 0.5
        sign = column(info, t, 3)
        for j in range(2 * chips):
            c, m = divmod(j, chips)
            span = slice(j * width, (j + 1) * width)
            turned_rows = []
            for s in range(2):
                source = moved.at[0, t] if s + j == 0 else gx.at[t, s, c, m]
                fields = [[source[f, i].astype(jnp.float32) for i in range(2)] for f in range(3)]
                if s == 1 and t == 0:
                    put = column(info, t, 4)[:EDGE] > 0.5
                    for f in range(3):
                        for i in range(2):
                            top = jnp.where(put, eg[c, m, f, i].astype(jnp.float32), fields[f][i][:EDGE])
                            fields[f][i] = (
                                jnp.concatenate([top, fields[f][i][EDGE:]], axis=0) if hb > EDGE else top
                            )
                turned_rows.append(wave_exponential(
                    fields, column(info, t, s), ky[:, span], (sine[t, s, :, span], cosine[t, s, :, span])
                ))
            for f in range(3):
                (re0, im0), (re1, im1) = turned_rows[0][f], turned_rows[1][f]
                for i, value in enumerate((
                    jnp.where(own_pair, re0, re0 + re1), jnp.where(own_pair, re1, sign * (im0 - im1))
                )):
                    rows_c[(i * 3 + f) * hb : (i * 3 + f + 1) * hb, span] = value.astype(jnp.bfloat16)
                for i, value in enumerate((
                    jnp.where(own_pair, -im0, -(im0 + im1)), jnp.where(own_pair, -im1, sign * (re0 - re1))
                )):
                    rows_s[(i * 3 + f) * hb : (i * 3 + f + 1) * hb, span] = value.astype(jnp.bfloat16)
        tile = min(length, max(block, 256))
        for y in range(0, length, tile):
            value = (
                jnp.dot(rows_c[...], ct[:, y : y + tile], preferred_element_type=jnp.float32)
                + jnp.dot(rows_s[...], st[:, y : y + tile], preferred_element_type=jnp.float32)
            ).astype(jnp.bfloat16)
            for b in range(tile // block):
                for i in range(2):
                    for f in range(3):
                        half[t, y // block + b, i * hb : (i + 1) * hb, f * block : (f + 1) * block] = (
                            value[(i * 3 + f) * hb : (i * 3 + f + 1) * hb, b * block : (b + 1) * block]
                        )
        for d in range(1, slots):
            to_grid(t, d).start()
        pltpu.make_async_copy(half.at[t, g], arr.at[t, g], l_s.at[t]).start()
    def to_rows(t, d):
        to = (g + d) % slots
        return remote(fh.at[t, to], ret.at[t, g], b_s.at[t, d], b_r.at[t, d], to, a)

    def sum_cores(t):
        return remote(stage.at[t, 1], rsin.at[t], d_s.at[t], d_r.at[t], g, partner)

    def sum_chips(t, m):
        return remote(xs.at[t, m], rx.at[t, m], y_s.at[t, m], y_r.at[t, m],
                      g, 2 * ((q + m) % chips) + core)

    def give(t):
        return remote(fin.at[t], other.at[t], gv_s.at[t], gv_r.at[t], slots - 1 - g, a)

    last = remote(fin.at[0, :, :, :EDGE], edge, le_s, le_r, edge_partner(g, slots), a)

    bring.wait()
    for t in range(chunks):
        for d in range(1, slots):
            to_grid(t, d).wait_recv()
        pltpu.make_async_copy(half.at[t, g], arr.at[t, g], l_s.at[t]).wait()
        together = max(1, 128 // (2 * hb))
        for p in range(0, slots, together):
            value = arr[t, p : p + together].astype(jnp.float32)
            value = value.reshape(together * 2 * hb, 3 * block)
            spot = p * 2 * hb
            arr_t[:, spot : spot + together * 2 * hb] = value.T.astype(jnp.bfloat16)
        depth = length // chunks
        for x in range(0, length, 256):
            value = jnp.dot(
                arr_t[...], packed[t * depth : (t + 1) * depth, x : x + 256],
                preferred_element_type=jnp.float32,
            )
            if t:
                value = value + grid[:, x : x + 256]
            if t < chunks - 1:
                grid[:, x : x + 256] = value
            else:
                value = value * (1.0 / length)
                east, north, height = (value[i * block : (i + 1) * block] for i in range(3))
                for k, pair in enumerate((
                    east * east, east * north, north * north, east * height, north * height
                )):
                    products[k * block : (k + 1) * block, x : x + 256] = pair.astype(jnp.bfloat16)
    for t in range(chunks):
        for k in range(0, depth, 256):
            value = lax.dot_general(
                packed[t * depth + k : t * depth + k + 256, :], products[...], DIMS_NT,
                preferred_element_type=jnp.float32,
            ).astype(jnp.bfloat16)
            for n in range(256 // (2 * hb)):
                fh[t, k // (2 * hb) + n] = value[n * 2 * hb : (n + 1) * 2 * hb]
        for d in range(1, slots):
            to_rows(t, d).start()
        pltpu.make_async_copy(fh.at[t, g], ret.at[t, g], m_s.at[t]).start()
    own_factors()

    @pl.when(low)
    def _():
        edge[...] = jnp.zeros_like(edge)

    for t in range(chunks):
        for d in range(1, slots):
            to_rows(t, d).wait_recv()
        pltpu.make_async_copy(fh.at[t, g], ret.at[t, g], m_s.at[t]).wait()
        for p in range(slots):
            for k in range(5):
                lhs[k * 2 * hb : (k + 1) * 2 * hb, p * block : (p + 1) * block] = (
                    ret[t, p, :, k * block : (k + 1) * block]
                )
        own_pair = column(info, t, 2) > 0.5
        sign, scale = column(info, t, 3), column(info, t, 5)
        for j in range(2 * chips):
            c, m = divmod(j, chips)
            span = slice(j * width, (j + 1) * width)
            by_c = lax.dot_general(lhs[...], ct[span, :], DIMS_NT, preferred_element_type=jnp.float32)
            by_s = lax.dot_general(lhs[...], st[span, :], DIMS_NT, preferred_element_type=jnp.float32)

            def part(values, k, i):
                return values[(2 * k + i) * hb : (2 * k + i + 1) * hb]

            for s in range(2):
                turn = scale * sign if s == 0 else -scale * sign
                real, imag = [], []
                for k in range(5):
                    rc, ic = part(by_c, k, 0), part(by_c, k, 1)
                    rs, iz = part(by_s, k, 0), part(by_s, k, 1)
                    real.append(jnp.where(own_pair, scale * (ic if s else rc), scale * rc + turn * iz))
                    imag.append(jnp.where(own_pair, -scale * (iz if s else rs), turn * ic - scale * rs))
                kx, kyj = column(info, t, s), ky[:, span]
                tendency = [
                    (kx * imag[u] + kyj * imag[v], -(kx * real[u] + kyj * real[v]))
                    for u, v in ((0, 1), (1, 2), (3, 4))
                ]
                back = wave_exponential(
                    tendency, kx, kyj, (-sine[t, s, :, span], cosine[t, s, :, span])
                )
                for f in range(3):
                    for i in range(2):
                        stage[t, c, m, s, f, i] = back[f][i].astype(jnp.bfloat16)
        sum_cores(t).start()
        sum_cores(t).wait_recv()
        for m in range(1, chips):
            xs[t, m] = (
                stage[t, 0, m].astype(jnp.float32) + rsin[t, m].astype(jnp.float32)
            ).astype(jnp.bfloat16)
            sum_chips(t, m).start()
        acc[...] = stage[t, 0, 0].astype(jnp.float32) + rsin[t, 0].astype(jnp.float32)
        for m in range(1, chips):
            sum_chips(t, m).wait_recv()
            acc[...] += rx[t, m].astype(jnp.float32)
        fin[t] = acc[1].astype(jnp.bfloat16)
        give(t).start()
        if t == 0:
            @pl.when(low)
            def _():
                last.start()
        own[t] = acc[0].astype(jnp.bfloat16)
    for t in range(chunks):
        give(t).wait_recv()

    @pl.when(high)
    def _():
        last.wait_recv()

    for t in range(chunks):
        exchange[t].wait_send()
        for s in range(2):
            for m in range(1, chips):
                over_chips(t, s, m).wait_send()
            for m in range(chips):
                over_cores(t, s, m).wait_send()
        for d in range(1, slots):
            to_grid(t, d).wait_send()

    @pl.when(high)
    def _():
        for copy in edges:
            copy.wait_send()


    for t in range(chunks):
        for d in range(1, slots):
            to_rows(t, d).wait_send()
        sum_cores(t).wait_send()
        for m in range(1, chips):
            sum_chips(t, m).wait_send()
        give(t).wait_send()

    @pl.when(low)
    def _():
        last.wait_send()


    for f in range(3):
        for i in range(2):
            rows = jnp.concatenate(
                [own[t, f, i] for t in range(chunks)] + [other[t, f, i] for t in range(chunks)]
                + [edge[f, i]], axis=0,
            )
            averaged = jnp.dot(back_rows[...], rows, preferred_element_type=jnp.float32)
            result[f, i] = state[f, i] + time_step * averaged
    fields = [[result[f, i] for i in range(2)] for f in range(3)]
    advanced = wave_exponential(fields, own_kx[...], ky[:, :width], (end_sine[...], end_cosine[...]))
    for f in range(3):
        for i in range(2):
            result[f, i] = advanced[f][i]


VMEM = pl.BlockSpec(memory_space=pltpu.VMEM)


def per_device(spectral_state, phase_index, weight_count):
    slots, owners = lax.axis_size("space"), lax.axis_size("avg")
    block, width = spectral_state.shape[2:]
    length, half = block * slots, block // 2
    chips = owners // 2
    chunks = max(1, half // CHUNK_ROWS)
    hb = half // chunks
    dims = (slots, chips, chunks, hb, width, block)
    g, a = lax.axis_index("space"), lax.axis_index("avg")
    q, core = a // 2, a % 2
    low = g < slots // 2
    phase = phase_index[0].astype(jnp.float32) * phase_step
    weight = weight_count[0].astype(jnp.float32) / (weight_scale * owners)

    m, c = jnp.arange(chips, dtype=jnp.int32), jnp.arange(2, dtype=jnp.int32)[:, None]
    order = (2 * ((q + m) % chips) + (core + c) % 2).reshape(-1)
    columns = (order[:, None] * width + jnp.arange(width, dtype=jnp.int32)).reshape(1, -1)
    ky = wave_of(columns, length)
    packed = jnp.asarray(packed_table(length, slots, chunks))

    base = jnp.where(low, 2 * half * g, 2 * half * (slots - 1 - g) + half)
    direct = base + jnp.arange(half, dtype=jnp.int32)
    mirror = jnp.where(direct == 0, length // 2, length - direct)
    first = wave_of(jnp.where(low, direct, mirror), length)
    second = wave_of(jnp.where(low, mirror, direct), length)
    ones = jnp.ones((half,), jnp.float32)
    start = (jnp.arange(half) == 0) & low
    info = jnp.stack([
        first, second, (direct == 0).astype(jnp.float32), jnp.where(low, ones, -ones),
        start.astype(jnp.float32), ones * (weight / length), ones, ones,
    ], axis=1).reshape(chunks, hb, 8)
    own_kx = wave_of(g * block + jnp.arange(block, dtype=jnp.int32)[:, None], length)

    r = np.arange(half)
    into = np.zeros((2, 2, half, block), np.float32)
    into[0, 0, r, r] = 1
    into[0, 1, r, half + r] = 1
    into[1, 0, r, half - r] = 1
    into[1, 1, r[1:], block - r[1:]] = 1
    into = jnp.asarray(into.reshape(2, block, block).astype(ml_dtypes.bfloat16))
    into = jnp.where(low, into[0], into[1])
    back = np.zeros((2, block, 2 * half + EDGE), np.float32)
    back[0, r, r] = 1
    back[0, half + r, half + r] = 1
    back[1, half - r, r] = 1
    back[1, block - r[1:], half + r[1:]] = 1
    back[1, 0, 2 * half] = 1
    back = jnp.asarray(back.astype(ml_dtypes.bfloat16))
    back = jnp.where(low, back[0], back[1])

    piece = (3, 2, hb, width)
    dma = pltpu.SemaphoreType.DMA
    vmem = lambda *shape: pltpu.VMEM(shape, jnp.bfloat16)
    wide = lambda *shape: pltpu.VMEM(shape, jnp.float32)
    return pl.pallas_call(
        functools.partial(step_kernel, dims),
        out_shape=jax.ShapeDtypeStruct(spectral_state.shape, jnp.float32),
        in_specs=[VMEM] * 10 + [pl.BlockSpec(memory_space=pl.ANY)],
        out_specs=VMEM,
        scratch_shapes=[
            vmem(2, chunks, *piece), vmem(3, 2, EDGE, width),
            vmem(chunks, 2, 2, chips, *piece), vmem(2, chips, 3, 2, EDGE, width),
            vmem(6 * hb, length), vmem(6 * hb, length),
            vmem(chunks, slots, 2 * hb, 3 * block), vmem(chunks, slots, 2 * hb, 3 * block),
            vmem(3 * block, length // chunks), wide(3 * block, length), vmem(5 * block, length),
            vmem(length, length), vmem(length, length), vmem(length, length),
            wide(chunks, 2, hb, length), wide(chunks, 2, hb, length),
            wide(block, width), wide(block, width),
            vmem(chunks, slots, 2 * hb, 5 * block), vmem(chunks, slots, 2 * hb, 5 * block),
            vmem(10 * hb, length),
            vmem(chunks, 2, chips, 2, *piece), vmem(chunks, chips, 2, *piece),
            wide(2, *piece), vmem(chunks, chips, 2, *piece), vmem(chunks, chips, 2, *piece),
            vmem(chunks, *piece), vmem(chunks, *piece), vmem(chunks, *piece),
            vmem(3, 2, EDGE, width),
            dma((chunks,)), dma((chunks,)),
            dma((2, chips)), dma((2, chips)),
            dma((chunks, 2, chips)), dma((chunks, 2, chips)),
            dma((chunks, 2, chips)), dma((chunks, 2, chips)),
            dma((chunks, slots)), dma((chunks, slots)), dma((chunks,)),
            dma((chunks, slots)), dma((chunks, slots)), dma((chunks,)),
            dma((chunks,)), dma((chunks,)),
            dma((chunks, chips)), dma((chunks, chips)),
            dma((chunks,)), dma((chunks,)),
            dma(()), dma(()), dma(()),
        ],
        compiler_params=pltpu.CompilerParams(
            collective_id=0, has_side_effects=True, vmem_limit_bytes=56 * 2**20
        ),
        name="averaged_step",
    )(spectral_state, into, back, info, ky, own_kx, phase.reshape(1, 1),
      *angle_tables(length, width, owners), packed)


CHUNK_ROWS = 32


def solution(mesh):
    in_specs = (P(None, None, "space", "avg"), P("avg"), P("avg"))
    out_specs = P(None, None, "space", "avg")
    return jax.shard_map(
        per_device, mesh=mesh, in_specs=in_specs, out_specs=out_specs, check_vma=False
    )
```

```python
import functools

import jax
import jax.numpy as jnp
import ml_dtypes
import numpy as np
from jax import lax
from jax.experimental import pallas as pl
from jax.experimental.pallas import tpu as pltpu
from jax.sharding import PartitionSpec as P

coriolis = 1.0
wave_speed = 6.0
phase_step = 0.25
time_step = 2.0
weight_scale = 4.0


def wave_of(positions, length):
    shifted = (positions + length // 2) % length - length // 2
    return shifted.astype(jnp.float32) * (2.0 / length)


def circle(products, length):
    angles = (products % length) * (2.0 * np.pi / length)
    return np.cos(angles).astype(np.float32), np.sin(angles).astype(np.float32)


def slot_base(slot, slots, half):
    return np.where(slot < slots // 2, 2 * half * slot, 2 * half * (slots - 1 - slot) + half)


def packed_table(length, slots, chunks):
    half = length // (2 * slots)
    rows = slot_base(np.arange(slots), slots, half)[:, None] + np.arange(half)
    cosine, sine = circle(rows[:, :, None] * np.arange(length), length)
    packed = np.stack([cosine, -sine], axis=1)
    packed[0, 1, 0] = circle(length // 2 * np.arange(length), length)[0]
    packed = packed.reshape(slots, 2, chunks, half // chunks, length).transpose(2, 0, 1, 3, 4)
    return packed.reshape(length, length).astype(ml_dtypes.bfloat16)


def turned(first, second):
    (c, s), (d, t) = first, second
    return c * d - s * t, s * d + c * t


def angle_tables(length, width, owners):
    y = np.arange(length)
    return [
        jnp.asarray(np.stack(circle(step * np.arange(count)[:, None] * y, length)))
        for step, count in ((width, owners), (FINE, width // FINE), (1, FINE))
    ]


def wave_operator(fields, kx, ky):
    (er, ei), (nr, ni), (hr, hi) = fields
    cx, cy = wave_speed * kx, wave_speed * ky
    return (
        (coriolis * nr + cx * hi, coriolis * ni - cx * hr),
        (cy * hi - coriolis * er, -coriolis * ei - cy * hr),
        (cx * ei + cy * ni, -(cx * er + cy * nr)),
    )


def wave_factors(kx, ky, phase):
    square = coriolis * coriolis + wave_speed * wave_speed * (kx * kx + ky * ky)
    frequency = jnp.sqrt(square)
    angle = frequency * phase
    return jnp.sin(angle) / frequency, (1.0 - jnp.cos(angle)) / square


def wave_exponential(fields, kx, ky, factors):
    sine, cosine = factors
    single = wave_operator(fields, kx, ky)
    double = wave_operator(single, kx, ky)
    return tuple(
        tuple(w + sine * a + cosine * b for w, a, b in zip(ws, one, two))
        for ws, one, two in zip(fields, single, double)
    )


def planes(fields):
    return tuple((fields[i, 0], fields[i, 1]) for i in range(fields.shape[0]))


MESH = pl.DeviceIdType.MESH
EDGE = 16
FINE = 16


def column(info, t, index):
    return info[t, :, index : index + 1]


def positions():
    g, a = lax.axis_index("space"), lax.axis_index("avg")
    return g, a, a // 2, a % 2


def edge_partner(g, slots):
    aligned = 1 - (g % (slots // 2) + slots // 2 - 1) // (slots // 2)
    return ((slots - g) % slots + aligned * (slots // 2)) % slots


def greet(slots, chips, edges):
    g, a, q, core = positions()
    barrier = pltpu.get_barrier_semaphore()
    peers = [((g + d) % slots, a) for d in range(1, slots)]
    peers += [(g, 2 * q + 1 - core)]
    peers += [(g, 2 * ((q + m) % chips) + core) for m in range(1, chips)]
    if edges:
        across = edge_partner(g, slots)
        peers += [
            (across, 2 * ((q + m) % chips) + (core + c) % 2)
            for c in range(2) for m in range(chips) if c or m
        ]
    for space, avg in peers:
        pl.semaphore_signal(
            barrier, inc=1, device_id={"space": space, "avg": avg}, device_id_type=MESH
        )
    pl.semaphore_wait(barrier, len(peers))


def sending(slots):
    return sorted(range(1, slots), key=lambda d: (-min(d, slots - d), d))


def remote(src, dst, send, recv, space, avg):
    return pltpu.make_async_remote_copy(
        src_ref=src, dst_ref=dst, send_sem=send, recv_sem=recv,
        device_id={"space": space, "avg": avg}, device_id_type=MESH,
    )


DIMS_NT = (((1,), (1,)), ((), ()))


def step_kernel(
    dims, state, into_rows, back_rows, info, ky, own_kx, phase, blocks, steps, fines, packed_hbm, result,
    moved, top, gx, eg, rows_c, rows_s, half, arr, arr_t, grid, products, packed, ct, st, sine, cosine,
    end_sine, end_cosine, fh, ret, lhs, stage, rsin, acc, xs, rx, fin, own, other, edge,
    ex_s, ex_r, eg_s, eg_r, x_s, x_r, c_s, c_r, a_s, a_r, l_s,
    b_s, b_r, m_s, d_s, d_r, y_s, y_r, gv_s, gv_r, le_s, le_r, bring_s,
):
    slots, chips, chunks, hb, width, block = dims
    length, reach = slots * block, block // 2
    g, a, q, core = positions()
    low, high = g < slots // 2, g >= slots // 2
    partner = 2 * q + 1 - core
    across = edge_partner(g, slots)
    side = g // (slots // 2)
    bring = pltpu.make_async_copy(packed_hbm, packed, bring_s)

    for f in range(3):
        for i in range(2):
            plane = state[f, i].astype(jnp.bfloat16)
            top[f, i] = plane[:EDGE]
            picked = jnp.dot(into_rows[side], plane, preferred_element_type=jnp.float32)
            picked = picked.astype(jnp.bfloat16)
            for s in range(2):
                for t in range(chunks):
                    spot = s * reach + t * hb
                    moved[s, t, f, i] = picked[spot : spot + hb]
    greet(slots, chips, True)

    def build_factors(unused):
        for t in range(chunks):
            for s in range(2):
                def one(j, carry, t=t, s=s):
                    span = pl.ds(pl.multiple_of(j * 256, 256), 256)
                    factors = wave_factors(column(info, t, s), ky[:, span], phase[...])
                    sine[t, s, :, span], cosine[t, s, :, span] = factors
                    return carry
                lax.fori_loop(0, length // 256, one, 0)

    def own_factors():
        end_sine[...], end_cosine[...] = wave_factors(own_kx[...], ky[:, :width], time_step)

    def build_tables():
        for c in range(2):
            for m in range(chips):
                owner = 2 * ((q + m) % chips) + (core + c) % 2
                first = (blocks[0, pl.ds(owner, 1), :], blocks[1, pl.ds(owner, 1), :])

                def one(h, carry, j=c * chips + m, first=first):
                    begin = turned(first, (steps[0, pl.ds(h, 1), :], steps[1, pl.ds(h, 1), :]))
                    cos_rows, sin_rows = turned(begin, (fines[0], fines[1]))
                    at = pl.ds(pl.multiple_of(j * width + h * FINE, FINE), FINE)
                    ct[at, :] = cos_rows.astype(jnp.bfloat16)
                    st[at, :] = sin_rows.astype(jnp.bfloat16)
                    return carry
                lax.fori_loop(0, width // FINE, one, 0)

    exchange = [
        remote(moved.at[1, t], gx.at[t, 1, 0, 0], ex_s.at[t], ex_r.at[t], slots - 1 - g, a)
        for t in range(chunks)
    ]
    edges = [
        remote(top, eg.at[c, m], eg_s.at[c, m], eg_r.at[c, m],
               across, 2 * ((q + chips - m) % chips) + (core + c) % 2)
        for c in range(2) for m in range(chips)
    ]

    def mine(t, s):
        return gx.at[t, 1, 0, 0] if s else moved.at[0, t]

    def over_chips(t, s, m):
        return remote(mine(t, s), gx.at[t, s, 0, m], x_s.at[t, s, m], x_r.at[t, s, m],
                      g, 2 * ((q + chips - m) % chips) + core)

    def over_cores(t, s, m):
        source = gx.at[t, s, 0, m] if m else mine(t, s)
        return remote(source, gx.at[t, s, 1, m], c_s.at[t, s, m], c_r.at[t, s, m], g, partner)

    def to_grid(t, d):
        to = (g + d) % slots
        return remote(half.at[t, to], arr.at[t, g], a_s.at[t, d], a_r.at[t, d], to, a)

    exchange[0].start()

    @pl.when(high)
    def _():
        for copy in edges:
            copy.start()
        eg[...] = jnp.zeros_like(eg)

    for t in range(1, chunks):
        exchange[t].start()
    for t in range(chunks):
        for m in range(1, chips):
            over_chips(t, 0, m).start()
        over_cores(t, 0, 0).start()
    bring.start()
    build_factors(0)
    build_tables()
    for t in range(chunks):
        for m in range(1, chips):
            over_chips(t, 0, m).wait_recv()
            over_cores(t, 0, m).start()
    for t in range(chunks):
        exchange[t].wait_recv()
        for m in range(1, chips):
            over_chips(t, 1, m).start()
        over_cores(t, 1, 0).start()
        for m in range(1, chips):
            over_chips(t, 1, m).wait_recv()
            over_cores(t, 1, m).start()
        if t == 0:
            @pl.when(low)
            def _():
                for copy in edges:
                    copy.wait_recv()
        for s in range(2):
            for m in range(chips):
                over_cores(t, s, m).wait_recv()
        own_pair = column(info, t, 2) > 0.5
        sign = column(info, t, 3)
        for j in range(2 * chips):
            c, m = divmod(j, chips)
            span = slice(j * width, (j + 1) * width)
            turned_rows = []
            for s in range(2):
                source = moved.at[0, t] if s + j == 0 else gx.at[t, s, c, m]
                fields = [[source[f, i].astype(jnp.float32) for i in range(2)] for f in range(3)]
                if s == 1 and t == 0:
                    put = column(info, t, 4)[:EDGE] > 0.5
                    for f in range(3):
                        for i in range(2):
                            top = jnp.where(put, eg[c, m, f, i].astype(jnp.float32), fields[f][i][:EDGE])
                            fields[f][i] = (
                                jnp.concatenate([top, fields[f][i][EDGE:]], axis=0) if hb > EDGE else top
                            )
                turned_rows.append(wave_exponential(
                    fields, column(info, t, s), ky[:, span], (sine[t, s, :, span], cosine[t, s, :, span])
                ))
            for f in range(3):
                (re0, im0), (re1, im1) = turned_rows[0][f], turned_rows[1][f]
                for i, value in enumerate((
                    jnp.where(own_pair, re0, re0 + re1), jnp.where(own_pair, re1, sign * (im0 - im1))
                )):
                    rows_c[(i * 3 + f) * hb : (i * 3 + f + 1) * hb, span] = value.astype(jnp.bfloat16)
                for i, value in enumerate((
                    jnp.where(own_pair, -im0, -(im0 + im1)), jnp.where(own_pair, -im1, sign * (re0 - re1))
                )):
                    rows_s[(i * 3 + f) * hb : (i * 3 + f + 1) * hb, span] = value.astype(jnp.bfloat16)
        tile = min(length, max(block, 256))
        for y in range(0, length, tile):
            value = (
                jnp.dot(rows_c[...], ct[:, y : y + tile], preferred_element_type=jnp.float32)
                + jnp.dot(rows_s[...], st[:, y : y + tile], preferred_element_type=jnp.float32)
            ).astype(jnp.bfloat16)
            for b in range(tile // block):
                for i in range(2):
                    for f in range(3):
                        half[t, y // block + b, i * hb : (i + 1) * hb, f * block : (f + 1) * block] = (
                            value[(i * 3 + f) * hb : (i * 3 + f + 1) * hb, b * block : (b + 1) * block]
                        )
        for d in sending(slots):
            to_grid(t, d).start()
        pltpu.make_async_copy(half.at[t, g], arr.at[t, g], l_s.at[t]).start()
    def to_rows(t, d):
        to = (g + d) % slots
        return remote(fh.at[t, to], ret.at[t, g], b_s.at[t, d], b_r.at[t, d], to, a)

    def sum_cores(t):
        return remote(stage.at[t, 1], rsin.at[t], d_s.at[t], d_r.at[t], g, partner)

    def sum_chips(t, m):
        return remote(xs.at[t, m], rx.at[t, m], y_s.at[t, m], y_r.at[t, m],
                      g, 2 * ((q + m) % chips) + core)

    def give(t):
        return remote(fin.at[t], other.at[t], gv_s.at[t], gv_r.at[t], slots - 1 - g, a)

    last = remote(fin.at[0, :, :, :EDGE], edge, le_s, le_r, edge_partner(g, slots), a)

    bring.wait()
    for t in range(chunks):
        for d in range(1, slots):
            to_grid(t, d).wait_recv()
        pltpu.make_async_copy(half.at[t, g], arr.at[t, g], l_s.at[t]).wait()
        together = max(1, 128 // (2 * hb))
        for p in range(0, slots, together):
            value = arr[t, p : p + together].astype(jnp.float32)
            value = value.reshape(together * 2 * hb, 3 * block)
            spot = p * 2 * hb
            arr_t[:, spot : spot + together * 2 * hb] = value.T.astype(jnp.bfloat16)
        depth = length // chunks
        for x in range(0, length, 256):
            value = jnp.dot(
                arr_t[...], packed[t * depth : (t + 1) * depth, x : x + 256],
                preferred_element_type=jnp.float32,
            )
            if t:
                value = value + grid[:, x : x + 256]
            if t < chunks - 1:
                grid[:, x : x + 256] = value
            else:
                value = value * (1.0 / length)
                east, north, height = (value[i * block : (i + 1) * block] for i in range(3))
                for k, pair in enumerate((
                    east * east, east * north, north * north, east * height, north * height
                )):
                    products[k * block : (k + 1) * block, x : x + 256] = pair.astype(jnp.bfloat16)
    for t in range(chunks):
        for k in range(0, depth, 256):
            value = lax.dot_general(
                packed[t * depth + k : t * depth + k + 256, :], products[...], DIMS_NT,
                preferred_element_type=jnp.float32,
            ).astype(jnp.bfloat16)
            for n in range(256 // (2 * hb)):
                fh[t, k // (2 * hb) + n] = value[n * 2 * hb : (n + 1) * 2 * hb]
        for d in sending(slots):
            to_rows(t, d).start()
        pltpu.make_async_copy(fh.at[t, g], ret.at[t, g], m_s.at[t]).start()
    own_factors()

    @pl.when(low)
    def _():
        edge[...] = jnp.zeros_like(edge)

    for t in range(chunks):
        for d in range(1, slots):
            to_rows(t, d).wait_recv()
        pltpu.make_async_copy(fh.at[t, g], ret.at[t, g], m_s.at[t]).wait()
        for p in range(slots):
            for k in range(5):
                lhs[k * 2 * hb : (k + 1) * 2 * hb, p * block : (p + 1) * block] = (
                    ret[t, p, :, k * block : (k + 1) * block]
                )
        own_pair = column(info, t, 2) > 0.5
        sign, scale = column(info, t, 3), column(info, t, 5)
        for j in range(2 * chips):
            c, m = divmod(j, chips)
            span = slice(j * width, (j + 1) * width)
            by_c = lax.dot_general(lhs[...], ct[span, :], DIMS_NT, preferred_element_type=jnp.float32)
            by_s = lax.dot_general(lhs[...], st[span, :], DIMS_NT, preferred_element_type=jnp.float32)

            def part(values, k, i):
                return values[(2 * k + i) * hb : (2 * k + i + 1) * hb]

            for s in range(2):
                turn = scale * sign if s == 0 else -scale * sign
                real, imag = [], []
                for k in range(5):
                    rc, ic = part(by_c, k, 0), part(by_c, k, 1)
                    rs, iz = part(by_s, k, 0), part(by_s, k, 1)
                    real.append(jnp.where(own_pair, scale * (ic if s else rc), scale * rc + turn * iz))
                    imag.append(jnp.where(own_pair, -scale * (iz if s else rs), turn * ic - scale * rs))
                kx, kyj = column(info, t, s), ky[:, span]
                tendency = [
                    (kx * imag[u] + kyj * imag[v], -(kx * real[u] + kyj * real[v]))
                    for u, v in ((0, 1), (1, 2), (3, 4))
                ]
                back = wave_exponential(
                    tendency, kx, kyj, (-sine[t, s, :, span], cosine[t, s, :, span])
                )
                for f in range(3):
                    for i in range(2):
                        stage[t, c, m, s, f, i] = back[f][i].astype(jnp.bfloat16)
        sum_cores(t).start()
        sum_cores(t).wait_recv()
        for m in range(1, chips):
            xs[t, m] = (
                stage[t, 0, m].astype(jnp.float32) + rsin[t, m].astype(jnp.float32)
            ).astype(jnp.bfloat16)
            sum_chips(t, m).start()
        acc[...] = stage[t, 0, 0].astype(jnp.float32) + rsin[t, 0].astype(jnp.float32)
        for m in range(1, chips):
            sum_chips(t, m).wait_recv()
            acc[...] += rx[t, m].astype(jnp.float32)
        fin[t] = acc[1].astype(jnp.bfloat16)
        give(t).start()
        if t == 0:
            @pl.when(low)
            def _():
                last.start()
        own[t] = acc[0].astype(jnp.bfloat16)
    for t in range(chunks):
        give(t).wait_recv()

    @pl.when(high)
    def _():
        last.wait_recv()

    for t in range(chunks):
        exchange[t].wait_send()
        for s in range(2):
            for m in range(1, chips):
                over_chips(t, s, m).wait_send()
            for m in range(chips):
                over_cores(t, s, m).wait_send()
        for d in range(1, slots):
            to_grid(t, d).wait_send()

    @pl.when(high)
    def _():
        for copy in edges:
            copy.wait_send()


    for t in range(chunks):
        for d in range(1, slots):
            to_rows(t, d).wait_send()
        sum_cores(t).wait_send()
        for m in range(1, chips):
            sum_chips(t, m).wait_send()
        give(t).wait_send()

    @pl.when(low)
    def _():
        last.wait_send()


    for f in range(3):
        for i in range(2):
            rows = jnp.concatenate(
                [own[t, f, i] for t in range(chunks)] + [other[t, f, i] for t in range(chunks)]
                + [edge[f, i]], axis=0,
            )
            averaged = jnp.dot(back_rows[side], rows, preferred_element_type=jnp.float32)
            result[f, i] = state[f, i] + time_step * averaged
    fields = [[result[f, i] for i in range(2)] for f in range(3)]
    advanced = wave_exponential(fields, own_kx[...], ky[:, :width], (end_sine[...], end_cosine[...]))
    for f in range(3):
        for i in range(2):
            result[f, i] = advanced[f][i]


VMEM = pl.BlockSpec(memory_space=pltpu.VMEM)


def per_device(spectral_state, phase_index, weight_count):
    slots, owners = lax.axis_size("space"), lax.axis_size("avg")
    block, width = spectral_state.shape[2:]
    length, half = block * slots, block // 2
    chips = owners // 2
    chunks = max(1, half // CHUNK_ROWS)
    hb = half // chunks
    dims = (slots, chips, chunks, hb, width, block)
    g, a = lax.axis_index("space"), lax.axis_index("avg")
    q, core = a // 2, a % 2
    low = g < slots // 2
    phase = phase_index[0].astype(jnp.float32) * phase_step
    weight = weight_count[0].astype(jnp.float32) / (weight_scale * owners)

    m, c = jnp.arange(chips, dtype=jnp.int32), jnp.arange(2, dtype=jnp.int32)[:, None]
    order = (2 * ((q + m) % chips) + (core + c) % 2).reshape(-1)
    columns = (order[:, None] * width + jnp.arange(width, dtype=jnp.int32)).reshape(1, -1)
    ky = wave_of(columns, length)
    packed = jnp.asarray(packed_table(length, slots, chunks))

    base = jnp.where(low, 2 * half * g, 2 * half * (slots - 1 - g) + half)
    direct = base + jnp.arange(half, dtype=jnp.int32)
    mirror = jnp.where(direct == 0, length // 2, length - direct)
    first = wave_of(jnp.where(low, direct, mirror), length)
    second = wave_of(jnp.where(low, mirror, direct), length)
    ones = jnp.ones((half,), jnp.float32)
    start = (jnp.arange(half) == 0) & low
    info = jnp.stack([
        first, second, (direct == 0).astype(jnp.float32), jnp.where(low, ones, -ones),
        start.astype(jnp.float32), ones * (weight / length), ones, ones,
    ], axis=1).reshape(chunks, hb, 8)
    own_kx = wave_of(g * block + jnp.arange(block, dtype=jnp.int32)[:, None], length)

    r = np.arange(half)
    into = np.zeros((2, 2, half, block), np.float32)
    into[0, 0, r, r] = 1
    into[0, 1, r, half + r] = 1
    into[1, 0, r, half - r] = 1
    into[1, 1, r[1:], block - r[1:]] = 1
    into = jnp.asarray(into.reshape(2, block, block).astype(ml_dtypes.bfloat16))
    back = np.zeros((2, block, 2 * half + EDGE), np.float32)
    back[0, r, r] = 1
    back[0, half + r, half + r] = 1
    back[1, half - r, r] = 1
    back[1, block - r[1:], half + r[1:]] = 1
    back[1, 0, 2 * half] = 1
    back = jnp.asarray(back.astype(ml_dtypes.bfloat16))

    piece = (3, 2, hb, width)
    dma = pltpu.SemaphoreType.DMA
    vmem = lambda *shape: pltpu.VMEM(shape, jnp.bfloat16)
    wide = lambda *shape: pltpu.VMEM(shape, jnp.float32)
    return pl.pallas_call(
        functools.partial(step_kernel, dims),
        out_shape=jax.ShapeDtypeStruct(spectral_state.shape, jnp.float32),
        in_specs=[VMEM] * 10 + [pl.BlockSpec(memory_space=pl.ANY)],
        out_specs=VMEM,
        scratch_shapes=[
            vmem(2, chunks, *piece), vmem(3, 2, EDGE, width),
            vmem(chunks, 2, 2, chips, *piece), vmem(2, chips, 3, 2, EDGE, width),
            vmem(6 * hb, length), vmem(6 * hb, length),
            vmem(chunks, slots, 2 * hb, 3 * block), vmem(chunks, slots, 2 * hb, 3 * block),
            vmem(3 * block, length // chunks), wide(3 * block, length), vmem(5 * block, length),
            vmem(length, length), vmem(length, length), vmem(length, length),
            wide(chunks, 2, hb, length), wide(chunks, 2, hb, length),
            wide(block, width), wide(block, width),
            vmem(chunks, slots, 2 * hb, 5 * block), vmem(chunks, slots, 2 * hb, 5 * block),
            vmem(10 * hb, length),
            vmem(chunks, 2, chips, 2, *piece), vmem(chunks, chips, 2, *piece),
            wide(2, *piece), vmem(chunks, chips, 2, *piece), vmem(chunks, chips, 2, *piece),
            vmem(chunks, *piece), vmem(chunks, *piece), vmem(chunks, *piece),
            vmem(3, 2, EDGE, width),
            dma((chunks,)), dma((chunks,)),
            dma((2, chips)), dma((2, chips)),
            dma((chunks, 2, chips)), dma((chunks, 2, chips)),
            dma((chunks, 2, chips)), dma((chunks, 2, chips)),
            dma((chunks, slots)), dma((chunks, slots)), dma((chunks,)),
            dma((chunks, slots)), dma((chunks, slots)), dma((chunks,)),
            dma((chunks,)), dma((chunks,)),
            dma((chunks, chips)), dma((chunks, chips)),
            dma((chunks,)), dma((chunks,)),
            dma(()), dma(()), dma(()),
        ],
        compiler_params=pltpu.CompilerParams(
            collective_id=0, has_side_effects=True, vmem_limit_bytes=56 * 2**20
        ),
        name="averaged_step",
    )(spectral_state, into, back, info, ky, own_kx, phase.reshape(1, 1),
      *angle_tables(length, width, owners), packed)


CHUNK_ROWS = 16


def solution(mesh):
    in_specs = (P(None, None, "space", "avg"), P("avg"), P("avg"))
    out_specs = P(None, None, "space", "avg")
    return jax.shard_map(
        per_device, mesh=mesh, in_specs=in_specs, out_specs=out_specs, check_vma=False
    )
```

```python
import functools

import jax
import jax.numpy as jnp
import ml_dtypes
import numpy as np
from jax import lax
from jax.experimental import pallas as pl
from jax.experimental.pallas import tpu as pltpu
from jax.sharding import PartitionSpec as P

coriolis = 1.0
wave_speed = 6.0
phase_step = 0.25
time_step = 2.0
weight_scale = 4.0


def wave_of(positions, length):
    shifted = (positions + length // 2) % length - length // 2
    return shifted.astype(jnp.float32) * (2.0 / length)


def circle(products, length):
    angles = (products % length) * (2.0 * np.pi / length)
    return np.cos(angles).astype(np.float32), np.sin(angles).astype(np.float32)


def slot_base(slot, slots, half):
    return np.where(slot < slots // 2, 2 * half * slot, 2 * half * (slots - 1 - slot) + half)


def packed_table(length, slots, chunks):
    half = length // (2 * slots)
    rows = slot_base(np.arange(slots), slots, half)[:, None] + np.arange(half)
    cosine, sine = circle(rows[:, :, None] * np.arange(length), length)
    packed = np.stack([cosine, -sine], axis=1)
    packed[0, 1, 0] = circle(length // 2 * np.arange(length), length)[0]
    packed = packed.reshape(slots, 2, chunks, half // chunks, length).transpose(2, 0, 1, 3, 4)
    return packed.reshape(length, length).astype(ml_dtypes.bfloat16)


def turned(first, second):
    (c, s), (d, t) = first, second
    return c * d - s * t, s * d + c * t


def angle_tables(length, width, owners):
    y = np.arange(length)
    return [
        jnp.asarray(np.stack(circle(step * np.arange(count)[:, None] * y, length)))
        for step, count in ((width, owners), (FINE, width // FINE), (1, FINE))
    ]


def wave_operator(fields, kx, ky):
    (er, ei), (nr, ni), (hr, hi) = fields
    cx, cy = wave_speed * kx, wave_speed * ky
    return (
        (coriolis * nr + cx * hi, coriolis * ni - cx * hr),
        (cy * hi - coriolis * er, -coriolis * ei - cy * hr),
        (cx * ei + cy * ni, -(cx * er + cy * nr)),
    )


def wave_factors(kx, ky, phase):
    square = coriolis * coriolis + wave_speed * wave_speed * (kx * kx + ky * ky)
    frequency = jnp.sqrt(square)
    angle = frequency * phase
    return jnp.sin(angle) / frequency, (1.0 - jnp.cos(angle)) / square


def wave_exponential(fields, kx, ky, factors):
    sine, cosine = factors
    single = wave_operator(fields, kx, ky)
    double = wave_operator(single, kx, ky)
    return tuple(
        tuple(w + sine * a + cosine * b for w, a, b in zip(ws, one, two))
        for ws, one, two in zip(fields, single, double)
    )


def planes(fields):
    return tuple((fields[i, 0], fields[i, 1]) for i in range(fields.shape[0]))


MESH = pl.DeviceIdType.MESH
EDGE = 16
FINE = 16


def column(info, t, index):
    return info[t, :, index : index + 1]


def positions():
    g, a = lax.axis_index("space"), lax.axis_index("avg")
    return g, a, a // 2, a % 2


def edge_partner(g, slots):
    aligned = 1 - (g % (slots // 2) + slots // 2 - 1) // (slots // 2)
    return ((slots - g) % slots + aligned * (slots // 2)) % slots


def greet(slots, chips, edges):
    g, a, q, core = positions()
    barrier = pltpu.get_barrier_semaphore()
    peers = [((g + d) % slots, a) for d in range(1, slots)]
    peers += [(g, 2 * q + 1 - core)]
    peers += [(g, 2 * ((q + m) % chips) + core) for m in range(1, chips)]
    if edges:
        across = edge_partner(g, slots)
        peers += [
            (across, 2 * ((q + m) % chips) + (core + c) % 2)
            for c in range(2) for m in range(chips) if c or m
        ]
    for space, avg in peers:
        pl.semaphore_signal(
            barrier, inc=1, device_id={"space": space, "avg": avg}, device_id_type=MESH
        )
    pl.semaphore_wait(barrier, len(peers))


def sending(slots):
    return sorted(range(1, slots), key=lambda d: (-min(d, slots - d), d))


def remote(src, dst, send, recv, space, avg):
    return pltpu.make_async_remote_copy(
        src_ref=src, dst_ref=dst, send_sem=send, recv_sem=recv,
        device_id={"space": space, "avg": avg}, device_id_type=MESH,
    )


DIMS_NT = (((1,), (1,)), ((), ()))


def step_kernel(
    dims, state, into_rows, back_rows, info, ky, own_kx, phase, blocks, steps, fines, packed_hbm, result,
    moved, top, gx, eg, rows_c, rows_s, half, arr, arr_t, grid, products, packed, ct, st, sine, cosine,
    end_sine, end_cosine, fh, ret, lhs, stage, rsin, acc, xs, rx, fin, own, other, edge,
    ex_s, ex_r, eg_s, eg_r, x_s, x_r, c_s, c_r, a_s, a_r, l_s,
    b_s, b_r, m_s, d_s, d_r, y_s, y_r, gv_s, gv_r, le_s, le_r, bring_s,
):
    slots, chips, chunks, hb, width, block = dims
    length, reach = slots * block, block // 2
    g, a, q, core = positions()
    low, high = g < slots // 2, g >= slots // 2
    partner = 2 * q + 1 - core
    across = edge_partner(g, slots)
    side = g // (slots // 2)
    bring = pltpu.make_async_copy(packed_hbm, packed, bring_s)

    for f in range(3):
        for i in range(2):
            plane = state[f, i].astype(jnp.bfloat16)
            top[f, i] = plane[:EDGE]
            picked = jnp.dot(into_rows[side], plane, preferred_element_type=jnp.float32)
            picked = picked.astype(jnp.bfloat16)
            for s in range(2):
                for t in range(chunks):
                    spot = s * reach + t * hb
                    moved[s, t, f, i] = picked[spot : spot + hb]
    greet(slots, chips, True)

    def build_factors(unused):
        for t in range(chunks):
            for s in range(2):
                def one(j, carry, t=t, s=s):
                    span = pl.ds(pl.multiple_of(j * 256, 256), 256)
                    factors = wave_factors(column(info, t, s), ky[:, span], phase[...])
                    sine[t, s, :, span], cosine[t, s, :, span] = factors
                    return carry
                lax.fori_loop(0, length // 256, one, 0)

    def own_factors():
        end_sine[...], end_cosine[...] = wave_factors(own_kx[...], ky[:, :width], time_step)

    def build_tables():
        for c in range(2):
            for m in range(chips):
                owner = 2 * ((q + m) % chips) + (core + c) % 2
                first = (blocks[0, pl.ds(owner, 1), :], blocks[1, pl.ds(owner, 1), :])

                def one(h, carry, j=c * chips + m, first=first):
                    begin = turned(first, (steps[0, pl.ds(h, 1), :], steps[1, pl.ds(h, 1), :]))
                    cos_rows, sin_rows = turned(begin, (fines[0], fines[1]))
                    at = pl.ds(pl.multiple_of(j * width + h * FINE, FINE), FINE)
                    ct[at, :] = cos_rows.astype(jnp.bfloat16)
                    st[at, :] = sin_rows.astype(jnp.bfloat16)
                    return carry
                lax.fori_loop(0, width // FINE, one, 0)

    exchange = [
        remote(moved.at[1, t], gx.at[t, 1, 0, 0], ex_s.at[t], ex_r.at[t], slots - 1 - g, a)
        for t in range(chunks)
    ]
    edges = [
        remote(top, eg.at[c, m], eg_s.at[c, m], eg_r.at[c, m],
               across, 2 * ((q + chips - m) % chips) + (core + c) % 2)
        for c in range(2) for m in range(chips)
    ]

    def mine(t, s):
        return gx.at[t, 1, 0, 0] if s else moved.at[0, t]

    def over_chips(t, s, m):
        return remote(mine(t, s), gx.at[t, s, 0, m], x_s.at[t, s, m], x_r.at[t, s, m],
                      g, 2 * ((q + chips - m) % chips) + core)

    def over_cores(t, s, m):
        source = gx.at[t, s, 0, m] if m else mine(t, s)
        return remote(source, gx.at[t, s, 1, m], c_s.at[t, s, m], c_r.at[t, s, m], g, partner)

    def to_grid(t, d):
        to = (g + d) % slots
        return remote(half.at[t, to], arr.at[t, g], a_s.at[t, d], a_r.at[t, d], to, a)

    exchange[0].start()

    @pl.when(high)
    def _():
        for copy in edges:
            copy.start()
        eg[...] = jnp.zeros_like(eg)

    for t in range(1, chunks):
        exchange[t].start()
    for t in range(chunks):
        for m in range(1, chips):
            over_chips(t, 0, m).start()
        over_cores(t, 0, 0).start()
    bring.start()
    build_factors(0)
    build_tables()
    for t in range(chunks):
        for m in range(1, chips):
            over_chips(t, 0, m).wait_recv()
            over_cores(t, 0, m).start()
    def spread(t):
        exchange[t].wait_recv()
        for m in range(1, chips):
            over_chips(t, 1, m).start()
        over_cores(t, 1, 0).start()

    spread(0)
    for t in range(chunks):
        for m in range(1, chips):
            over_chips(t, 1, m).wait_recv()
            over_cores(t, 1, m).start()
        if t + 1 < chunks:
            spread(t + 1)
        if t == 0:
            @pl.when(low)
            def _():
                for copy in edges:
                    copy.wait_recv()
        for s in range(2):
            for m in range(chips):
                over_cores(t, s, m).wait_recv()
        own_pair = column(info, t, 2) > 0.5
        sign = column(info, t, 3)
        for j in range(2 * chips):
            c, m = divmod(j, chips)
            span = slice(j * width, (j + 1) * width)
            turned_rows = []
            for s in range(2):
                source = moved.at[0, t] if s + j == 0 else gx.at[t, s, c, m]
                fields = [[source[f, i].astype(jnp.float32) for i in range(2)] for f in range(3)]
                if s == 1 and t == 0:
                    put = column(info, t, 4)[:EDGE] > 0.5
                    for f in range(3):
                        for i in range(2):
                            top = jnp.where(put, eg[c, m, f, i].astype(jnp.float32), fields[f][i][:EDGE])
                            fields[f][i] = (
                                jnp.concatenate([top, fields[f][i][EDGE:]], axis=0) if hb > EDGE else top
                            )
                turned_rows.append(wave_exponential(
                    fields, column(info, t, s), ky[:, span], (sine[t, s, :, span], cosine[t, s, :, span])
                ))
            for f in range(3):
                (re0, im0), (re1, im1) = turned_rows[0][f], turned_rows[1][f]
                for i, value in enumerate((
                    jnp.where(own_pair, re0, re0 + re1), jnp.where(own_pair, re1, sign * (im0 - im1))
                )):
                    rows_c[(i * 3 + f) * hb : (i * 3 + f + 1) * hb, span] = value.astype(jnp.bfloat16)
                for i, value in enumerate((
                    jnp.where(own_pair, -im0, -(im0 + im1)), jnp.where(own_pair, -im1, sign * (re0 - re1))
                )):
                    rows_s[(i * 3 + f) * hb : (i * 3 + f + 1) * hb, span] = value.astype(jnp.bfloat16)
        tile = min(length, max(block, 256))
        for y in range(0, length, tile):
            value = (
                jnp.dot(rows_c[...], ct[:, y : y + tile], preferred_element_type=jnp.float32)
                + jnp.dot(rows_s[...], st[:, y : y + tile], preferred_element_type=jnp.float32)
            ).astype(jnp.bfloat16)
            for b in range(tile // block):
                for i in range(2):
                    for f in range(3):
                        half[t, y // block + b, i * hb : (i + 1) * hb, f * block : (f + 1) * block] = (
                            value[(i * 3 + f) * hb : (i * 3 + f + 1) * hb, b * block : (b + 1) * block]
                        )
        for d in sending(slots):
            to_grid(t, d).start()
        pltpu.make_async_copy(half.at[t, g], arr.at[t, g], l_s.at[t]).start()
    def to_rows(t, d):
        to = (g + d) % slots
        return remote(fh.at[t, to], ret.at[t, g], b_s.at[t, d], b_r.at[t, d], to, a)

    def sum_cores(t):
        return remote(stage.at[t, 1], rsin.at[t], d_s.at[t], d_r.at[t], g, partner)

    def sum_chips(t, m):
        return remote(xs.at[t, m], rx.at[t, m], y_s.at[t, m], y_r.at[t, m],
                      g, 2 * ((q + m) % chips) + core)

    def give(t):
        return remote(fin.at[t], other.at[t], gv_s.at[t], gv_r.at[t], slots - 1 - g, a)

    last = remote(fin.at[0, :, :, :EDGE], edge, le_s, le_r, edge_partner(g, slots), a)

    bring.wait()
    for t in range(chunks):
        for d in range(1, slots):
            to_grid(t, d).wait_recv()
        pltpu.make_async_copy(half.at[t, g], arr.at[t, g], l_s.at[t]).wait()
        together = max(1, 128 // (2 * hb))
        for p in range(0, slots, together):
            value = arr[t, p : p + together].astype(jnp.float32)
            value = value.reshape(together * 2 * hb, 3 * block)
            spot = p * 2 * hb
            arr_t[:, spot : spot + together * 2 * hb] = value.T.astype(jnp.bfloat16)
        depth = length // chunks
        for x in range(0, length, 256):
            value = jnp.dot(
                arr_t[...], packed[t * depth : (t + 1) * depth, x : x + 256],
                preferred_element_type=jnp.float32,
            )
            if t:
                value = value + grid[:, x : x + 256]
            if t < chunks - 1:
                grid[:, x : x + 256] = value
            else:
                value = value * (1.0 / length)
                east, north, height = (value[i * block : (i + 1) * block] for i in range(3))
                for k, pair in enumerate((
                    east * east, east * north, north * north, east * height, north * height
                )):
                    products[k * block : (k + 1) * block, x : x + 256] = pair.astype(jnp.bfloat16)
    for t in range(chunks):
        for k in range(0, depth, 256):
            value = lax.dot_general(
                packed[t * depth + k : t * depth + k + 256, :], products[...], DIMS_NT,
                preferred_element_type=jnp.float32,
            ).astype(jnp.bfloat16)
            for n in range(256 // (2 * hb)):
                fh[t, k // (2 * hb) + n] = value[n * 2 * hb : (n + 1) * 2 * hb]
        for d in sending(slots):
            to_rows(t, d).start()
        pltpu.make_async_copy(fh.at[t, g], ret.at[t, g], m_s.at[t]).start()
    own_factors()

    @pl.when(low)
    def _():
        edge[...] = jnp.zeros_like(edge)

    def finish(t):
        for m in range(1, chips):
            sum_chips(t, m).wait_recv()
            acc[...] += rx[t, m].astype(jnp.float32)
        fin[t] = acc[1].astype(jnp.bfloat16)
        give(t).start()
        if t == 0:
            @pl.when(low)
            def _():
                last.start()
        own[t] = acc[0].astype(jnp.bfloat16)

    for t in range(chunks):
        for d in range(1, slots):
            to_rows(t, d).wait_recv()
        pltpu.make_async_copy(fh.at[t, g], ret.at[t, g], m_s.at[t]).wait()
        for p in range(slots):
            for k in range(5):
                lhs[k * 2 * hb : (k + 1) * 2 * hb, p * block : (p + 1) * block] = (
                    ret[t, p, :, k * block : (k + 1) * block]
                )
        own_pair = column(info, t, 2) > 0.5
        sign, scale = column(info, t, 3), column(info, t, 5)
        for j in range(2 * chips):
            c, m = divmod(j, chips)
            span = slice(j * width, (j + 1) * width)
            by_c = lax.dot_general(lhs[...], ct[span, :], DIMS_NT, preferred_element_type=jnp.float32)
            by_s = lax.dot_general(lhs[...], st[span, :], DIMS_NT, preferred_element_type=jnp.float32)

            def part(values, k, i):
                return values[(2 * k + i) * hb : (2 * k + i + 1) * hb]

            for s in range(2):
                turn = scale * sign if s == 0 else -scale * sign
                real, imag = [], []
                for k in range(5):
                    rc, ic = part(by_c, k, 0), part(by_c, k, 1)
                    rs, iz = part(by_s, k, 0), part(by_s, k, 1)
                    real.append(jnp.where(own_pair, scale * (ic if s else rc), scale * rc + turn * iz))
                    imag.append(jnp.where(own_pair, -scale * (iz if s else rs), turn * ic - scale * rs))
                kx, kyj = column(info, t, s), ky[:, span]
                tendency = [
                    (kx * imag[u] + kyj * imag[v], -(kx * real[u] + kyj * real[v]))
                    for u, v in ((0, 1), (1, 2), (3, 4))
                ]
                back = wave_exponential(
                    tendency, kx, kyj, (-sine[t, s, :, span], cosine[t, s, :, span])
                )
                for f in range(3):
                    for i in range(2):
                        stage[t, c, m, s, f, i] = back[f][i].astype(jnp.bfloat16)
        sum_cores(t).start()
        if t:
            finish(t - 1)
        sum_cores(t).wait_recv()
        for m in range(1, chips):
            xs[t, m] = (
                stage[t, 0, m].astype(jnp.float32) + rsin[t, m].astype(jnp.float32)
            ).astype(jnp.bfloat16)
            sum_chips(t, m).start()
        acc[...] = stage[t, 0, 0].astype(jnp.float32) + rsin[t, 0].astype(jnp.float32)
    finish(chunks - 1)
    for t in range(chunks):
        give(t).wait_recv()

    @pl.when(high)
    def _():
        last.wait_recv()

    for t in range(chunks):
        exchange[t].wait_send()
        for s in range(2):
            for m in range(1, chips):
                over_chips(t, s, m).wait_send()
            for m in range(chips):
                over_cores(t, s, m).wait_send()
        for d in range(1, slots):
            to_grid(t, d).wait_send()

    @pl.when(high)
    def _():
        for copy in edges:
            copy.wait_send()


    for t in range(chunks):
        for d in range(1, slots):
            to_rows(t, d).wait_send()
        sum_cores(t).wait_send()
        for m in range(1, chips):
            sum_chips(t, m).wait_send()
        give(t).wait_send()

    @pl.when(low)
    def _():
        last.wait_send()


    for f in range(3):
        for i in range(2):
            rows = jnp.concatenate(
                [own[t, f, i] for t in range(chunks)] + [other[t, f, i] for t in range(chunks)]
                + [edge[f, i]], axis=0,
            )
            averaged = jnp.dot(back_rows[side], rows, preferred_element_type=jnp.float32)
            result[f, i] = state[f, i] + time_step * averaged
    fields = [[result[f, i] for i in range(2)] for f in range(3)]
    advanced = wave_exponential(fields, own_kx[...], ky[:, :width], (end_sine[...], end_cosine[...]))
    for f in range(3):
        for i in range(2):
            result[f, i] = advanced[f][i]


VMEM = pl.BlockSpec(memory_space=pltpu.VMEM)


def per_device(spectral_state, phase_index, weight_count):
    slots, owners = lax.axis_size("space"), lax.axis_size("avg")
    block, width = spectral_state.shape[2:]
    length, half = block * slots, block // 2
    chips = owners // 2
    chunks = max(1, half // CHUNK_ROWS)
    hb = half // chunks
    dims = (slots, chips, chunks, hb, width, block)
    g, a = lax.axis_index("space"), lax.axis_index("avg")
    q, core = a // 2, a % 2
    low = g < slots // 2
    phase = phase_index[0].astype(jnp.float32) * phase_step
    weight = weight_count[0].astype(jnp.float32) / (weight_scale * owners)

    m, c = jnp.arange(chips, dtype=jnp.int32), jnp.arange(2, dtype=jnp.int32)[:, None]
    order = (2 * ((q + m) % chips) + (core + c) % 2).reshape(-1)
    columns = (order[:, None] * width + jnp.arange(width, dtype=jnp.int32)).reshape(1, -1)
    ky = wave_of(columns, length)
    packed = jnp.asarray(packed_table(length, slots, chunks))

    base = jnp.where(low, 2 * half * g, 2 * half * (slots - 1 - g) + half)
    direct = base + jnp.arange(half, dtype=jnp.int32)
    mirror = jnp.where(direct == 0, length // 2, length - direct)
    first = wave_of(jnp.where(low, direct, mirror), length)
    second = wave_of(jnp.where(low, mirror, direct), length)
    ones = jnp.ones((half,), jnp.float32)
    start = (jnp.arange(half) == 0) & low
    info = jnp.stack([
        first, second, (direct == 0).astype(jnp.float32), jnp.where(low, ones, -ones),
        start.astype(jnp.float32), ones * (weight / length), ones, ones,
    ], axis=1).reshape(chunks, hb, 8)
    own_kx = wave_of(g * block + jnp.arange(block, dtype=jnp.int32)[:, None], length)

    r = np.arange(half)
    into = np.zeros((2, 2, half, block), np.float32)
    into[0, 0, r, r] = 1
    into[0, 1, r, half + r] = 1
    into[1, 0, r, half - r] = 1
    into[1, 1, r[1:], block - r[1:]] = 1
    into = jnp.asarray(into.reshape(2, block, block).astype(ml_dtypes.bfloat16))
    back = np.zeros((2, block, 2 * half + EDGE), np.float32)
    back[0, r, r] = 1
    back[0, half + r, half + r] = 1
    back[1, half - r, r] = 1
    back[1, block - r[1:], half + r[1:]] = 1
    back[1, 0, 2 * half] = 1
    back = jnp.asarray(back.astype(ml_dtypes.bfloat16))

    piece = (3, 2, hb, width)
    dma = pltpu.SemaphoreType.DMA
    vmem = lambda *shape: pltpu.VMEM(shape, jnp.bfloat16)
    wide = lambda *shape: pltpu.VMEM(shape, jnp.float32)
    return pl.pallas_call(
        functools.partial(step_kernel, dims),
        out_shape=jax.ShapeDtypeStruct(spectral_state.shape, jnp.float32),
        in_specs=[VMEM] * 10 + [pl.BlockSpec(memory_space=pl.ANY)],
        out_specs=VMEM,
        scratch_shapes=[
            vmem(2, chunks, *piece), vmem(3, 2, EDGE, width),
            vmem(chunks, 2, 2, chips, *piece), vmem(2, chips, 3, 2, EDGE, width),
            vmem(6 * hb, length), vmem(6 * hb, length),
            vmem(chunks, slots, 2 * hb, 3 * block), vmem(chunks, slots, 2 * hb, 3 * block),
            vmem(3 * block, length // chunks), wide(3 * block, length), vmem(5 * block, length),
            vmem(length, length), vmem(length, length), vmem(length, length),
            wide(chunks, 2, hb, length), wide(chunks, 2, hb, length),
            wide(block, width), wide(block, width),
            vmem(chunks, slots, 2 * hb, 5 * block), vmem(chunks, slots, 2 * hb, 5 * block),
            vmem(10 * hb, length),
            vmem(chunks, 2, chips, 2, *piece), vmem(chunks, chips, 2, *piece),
            wide(2, *piece), vmem(chunks, chips, 2, *piece), vmem(chunks, chips, 2, *piece),
            vmem(chunks, *piece), vmem(chunks, *piece), vmem(chunks, *piece),
            vmem(3, 2, EDGE, width),
            dma((chunks,)), dma((chunks,)),
            dma((2, chips)), dma((2, chips)),
            dma((chunks, 2, chips)), dma((chunks, 2, chips)),
            dma((chunks, 2, chips)), dma((chunks, 2, chips)),
            dma((chunks, slots)), dma((chunks, slots)), dma((chunks,)),
            dma((chunks, slots)), dma((chunks, slots)), dma((chunks,)),
            dma((chunks,)), dma((chunks,)),
            dma((chunks, chips)), dma((chunks, chips)),
            dma((chunks,)), dma((chunks,)),
            dma(()), dma(()), dma(()),
        ],
        compiler_params=pltpu.CompilerParams(
            collective_id=0, has_side_effects=True, vmem_limit_bytes=56 * 2**20
        ),
        name="averaged_step",
    )(spectral_state, into, back, info, ky, own_kx, phase.reshape(1, 1),
      *angle_tables(length, width, owners), packed)


CHUNK_ROWS = 16


def solution(mesh):
    in_specs = (P(None, None, "space", "avg"), P("avg"), P("avg"))
    out_specs = P(None, None, "space", "avg")
    return jax.shard_map(
        per_device, mesh=mesh, in_specs=in_specs, out_specs=out_specs, check_vma=False
    )
```
